256 devices in a mesh: block: 8 (over z), tile: 32 (over x, y, core).
Axes of the slice: x: 4, y: 4, z: 8, core: 2. Of those that a mesh axis runs over, the one named last changes fastest.
Arguments:
- acts: bfloat16 [16, 32, 64, 384], P('block', 'tile'), may hold values from -6 to 6
- gamma: float32 [384], replicated, may hold values from 0.25 to 1.75
- beta: float32 [384], replicated, may hold values from -3 to 3
- weights: bfloat16 [384, 27, 192], P('tile'), may hold values from -0.0625 to 0.0625
- cotangent: bfloat16 [16, 64, 128, 192], P('block', 'tile'), may hold values from -6 to 6
Outputs:
- d_acts: bfloat16 [16, 32, 64, 384], P('block', 'tile')
- d_weights: float32 [384, 27, 192], P('tile')
The draws below stay inside these ranges and needn't reach their ends.
All inputs are finite; a program needn't handle non-finite values.
Results may differ from the reference program's by a relative error of at most 0.0029.
Values may be sent and summed in bfloat16 or wider, within the bound.
A program may use at most 128 MiB of HBM per device.

```python
import jax
import jax.numpy as jnp
from jax import lax

C_IN = 384
C_OUT = 192
GROUPS = 32
TAPS = 27
WL = 64
FRAMES = 16
HEIGHT = 32


def block_levels(key, shape, pieces, least, largest):
    factor_of = 1.0
    for dim, blocks in pieces:
        draws = jax.random.uniform(jax.random.fold_in(jax.random.fold_in(key, 6), dim), (blocks,), jnp.float32, least / len(pieces), largest / len(pieces))
        factor_of = factor_of * jnp.repeat(jnp.exp(draws), shape[dim] // blocks).reshape((-1,) + (1,) * (len(shape) - 1 - dim))
    return factor_of


def noise(rng, shape, deviation, reach, cuts=(), kind=jnp.bfloat16):
    gain = block_levels(rng, shape, cuts, -0.22, 0.18) if cuts else 1.0
    array = jax.random.normal(rng, shape, jnp.float32) * deviation * gain
    return jnp.minimum(jnp.maximum(array, -reach), reach).astype(kind)


def setup_inputs(seed: int = 0) -> dict:
    seeds = jax.random.split(jax.random.key(seed), 6)
    acts = noise(seeds[0], (FRAMES, HEIGHT, WL, C_IN), 1.0, 6.0, ((0, 8), (1, 32)))
    gamma = jnp.clip(1.0 + 0.15 * jax.random.normal(seeds[1], (C_IN,), jnp.float32), 0.25, 1.75)
    beta = noise(seeds[2], (C_IN,), 0.5, 3.0, (), jnp.float32)
    weights = noise(seeds[3], (C_IN, TAPS, C_OUT), (27 * C_IN) ** -0.5, 0.0625, ((0, 32),))
    cotangent = noise(seeds[4], (FRAMES, 2 * HEIGHT, 2 * WL, C_OUT), 1.0, 6.0, ((0, 8), (1, 32)))
    return dict(acts=acts, gamma=gamma, beta=beta, weights=weights, cotangent=cotangent)


norm_eps = 1e-06

def group_totals(values, frames, per_group):
    return lax.optimization_barrier(jnp.sum(values, axis=(1, 2))).reshape(frames, GROUPS, per_group).sum(-1)

def reference(acts, gamma, beta, weights, cotangent):
    frames, height, width, channels = acts.shape
    per_group = channels // GROUPS
    group_size = height * width * per_group
    acts_wide = acts.astype(jnp.float32)
    stat_sum = group_totals(acts_wide, frames, per_group)
    stat_sq = group_totals(acts_wide * acts_wide, frames, per_group)
    group_mean = stat_sum / group_size
    inv_std = lax.rsqrt(stat_sq / group_size - group_mean * group_mean + norm_eps)
    mean_chan = jnp.repeat(group_mean, per_group, axis=1)[:, None, None, :]
    inv_chan = jnp.repeat(inv_std, per_group, axis=1)[:, None, None, :]
    normed = (acts_wide - mean_chan) * inv_chan
    shifted = normed * gamma + beta
    gate_value = jax.nn.sigmoid(shifted)
    hidden = (shifted * gate_value).astype(jnp.bfloat16)
    upsampled = jnp.repeat(jnp.repeat(hidden, 2, axis=1), 2, axis=2)
    upsampled = jnp.pad(upsampled, ((2, 0), (1, 1), (1, 1), (0, 0)))
    grad_field = jnp.pad(cotangent, ((0, 2), (1, 1), (1, 1), (0, 0)))
    up_rows = 2 * height
    up_cols = 2 * width
    num_cells = frames * up_rows * up_cols
    flat_grads = cotangent.reshape(num_cells, -1)
    act_grad = jnp.zeros((frames, height, width, channels), jnp.float32)
    weight_list = []
    for tap in range(27):
        tap_t = tap // 9
        tap_h = tap // 3 % 3
        tap_w = tap % 3
        window_g = grad_field[2 - tap_t:2 - tap_t + frames, 2 - tap_h:2 - tap_h + up_rows, 2 - tap_w:2 - tap_w + up_cols]
        window_g = window_g.reshape(num_cells, -1)
        back_grad = jnp.dot(window_g, weights[:, tap, :].T, preferred_element_type=jnp.float32)
        act_grad = act_grad + back_grad.reshape(frames, height, 2, width, 2, channels).sum(axis=(2, 4))
        window_h = upsampled[tap_t:tap_t + frames, tap_h:tap_h + up_rows, tap_w:tap_w + up_cols]
        window_h = window_h.reshape(num_cells, channels)
        weight_list.append(jnp.dot(window_h.T, flat_grads, preferred_element_type=jnp.float32))
    d_weights = jnp.stack(weight_list, 1)
    silu_slope = gate_value * (1.0 + shifted * (1.0 - gate_value))
    norm_grad = act_grad * silu_slope * gamma
    first_sum = group_totals(norm_grad, frames, per_group)
    second_sum = group_totals(norm_grad * normed, frames, per_group)
    first_chan = jnp.repeat(first_sum / group_size, per_group, axis=1)[:, None, None, :]
    second_chan = jnp.repeat(second_sum / group_size, per_group, axis=1)[:, None, None, :]
    d_acts = (inv_chan * (norm_grad - first_chan - normed * second_chan)).astype(jnp.bfloat16)
    return (d_acts, d_weights)
```

```python
import jax
import jax.numpy as jnp
from jax import lax
from jax.experimental import pallas as pl
from jax.experimental.pallas import tpu as pltpu
from jax.sharding import PartitionSpec as P

GROUPS = 32
NORM_EPS = 1e-06
MESH = pl.DeviceIdType.MESH
BF = jnp.bfloat16
F32 = jnp.float32
HALF = 896
CUT = 512
NCOPY = 96
VMEM = pltpu.VMEM


def rows_iota(shape, dim):
    return lax.broadcasted_iota(jnp.int32, shape, dim)


def div12(v):
    return (v * 5462) >> 16


def kernel(n_norm, acts, cot, w, gamma, beta, dacts, dw,
           actbuf, cotbuf, stat_out, stat_in, ghi, glo,
           wy, wx, dpart, sb, rp1, rp2, ra, rb, sm1, sm2,
           dpart2, sb2, rq1, rq2, ra2, rb2, sn1, sn2,
           fin, finb, zin, zred, zout, dsend, drecv, perm_scr, send_sem, recv_sem):
    z = lax.axis_index("block")
    tile = lax.axis_index("tile")
    core = lax.rem(tile, 2)
    q = lax.div(tile, 2)
    y = lax.rem(q, 4)
    x = lax.div(q, 4)

    def chip(cx, cy):
        return {"tile": (cx * 4 + cy) * 2 + core}

    partner = {"tile": tile + 1 - 2 * core}
    outer = {"tile": lax.rem(tile + 2 * core - 1 + 32, 32)}
    xp, xm = chip(lax.rem(x + 1, 4), y), chip(lax.rem(x + 3, 4), y)
    yp, ym = chip(x, lax.rem(y + 1, 4)), chip(x, lax.rem(y + 3, 4))
    plane = [{"tile": lax.rem(q + d, 16) * 2 + core} for d in range(1, 16)]
    column = [{"block": lax.rem(z + k, 8)} for k in range(1, 8)]
    before = {"block": lax.rem(z + 7, 8)}

    copies = []

    def copy(src, dst, device):
        k = len(copies)
        c = pltpu.make_async_remote_copy(
            src_ref=src, dst_ref=dst, send_sem=send_sem.at[k], recv_sem=recv_sem.at[k],
            device_id=device, device_id_type=MESH)
        copies.append(c)
        c.start()
        return c

    barrier = pltpu.get_barrier_semaphore()
    friends = plane + column + [partner, outer]
    for dev in friends:
        pl.semaphore_signal(barrier, inc=1, device_id=dev, device_id_type=MESH)
    pl.semaphore_wait(barrier, len(friends))

    own = pl.ds(1 + 2 * core, 2)
    c_act = copy(acts, actbuf.at[:, core], partner)
    c_z = copy(cot, cotbuf.at[pl.ds(2, 2), own], before)
    c_pair = copy(cot, cotbuf.at[pl.ds(0, 2), own], partner)
    c_edge = copy(cot.at[:, core], cotbuf.at[pl.ds(0, 2), 5 * (1 - core)], outer)

    places = ((y, yp, ym, x, xp, xm), (x, xp, xm, y, yp, ym))

    def gather_start(buf, p, plus, minus):
        return copy(buf.at[p], buf.at[p], plus), copy(buf.at[p], buf.at[p], minus)

    def gather_forward(buf, p, plus, minus, pair):
        pair[0].wait_recv()
        low = lax.rem(p + 3, 4)
        f1 = copy(buf.at[low, :, :, pl.ds(0, CUT)], buf.at[low, :, :, pl.ds(0, CUT)], plus)
        pair[1].wait_recv()
        high = lax.rem(p + 1, 4)
        f2 = copy(buf.at[high, :, :, pl.ds(CUT, HALF - CUT)],
                  buf.at[high, :, :, pl.ds(CUT, HALF - CUT)], minus)
        return f1, f2

    first = []
    for h in range(2):
        p, plus, minus = places[h][:3]
        wy[h, p] = w[h]
        first.append(gather_start(wy.at[h], p, plus, minus))

    actbuf[:, core] = acts[...]
    cotbuf[0:2, own] = cot[...]
    row = rows_iota((192, 384), 0)
    col = rows_iota((192, 384), 1)
    blk = div12(row)
    pick = col == row + 12 * blk + 12 * core
    pick_bf = jnp.where(pick, 1.0, 0.0).astype(BF)
    gcol = jnp.sum(jnp.where(pick, gamma[...], 0.0), axis=1, keepdims=True)
    bcol = jnp.sum(jnp.where(pick, beta[...], 0.0), axis=1, keepdims=True)
    member = rows_iota((192, 128), 1) == div12(rows_iota((192, 128), 0))
    c_act.wait_recv()
    xt = lax.dot_general(pick_bf, actbuf[...].reshape(256, 384), (((1,), (1,)), ((), ())),
                         preferred_element_type=F32)

    def group_sums(u, v):
        lines = []
        for value in (u, v):
            for t in range(2):
                c = jnp.sum(value[:, 128 * t:128 * t + 128], axis=1, keepdims=True)
                lines.append(jnp.sum(jnp.where(member, c, 0.0), axis=0, keepdims=True))
        return jnp.concatenate(lines + [jnp.zeros((4, 128), F32)], axis=0)

    def spread(line):
        return jnp.sum(jnp.where(member, line, 0.0), axis=1, keepdims=True)

    def stats_start(k, total):
        stat_out[k] = total
        return [copy(stat_out.at[k], stat_in.at[k, d], plane[d]) for d in range(15)]

    def stats_end(k, total, cs):
        for d in range(15):
            cs[d].wait_recv()
            total = total + stat_in[k, d]
        return total

    tot1 = group_sums(xt, xt * xt)
    s1 = stats_start(0, tot1)

    second = [gather_forward(wy.at[h], *places[h][:3], first[h]) for h in range(2)]

    c_edge.wait_recv()
    line = 5 * core
    c_edge_f = copy(cotbuf.at[pl.ds(0, 2), line], cotbuf.at[pl.ds(0, 2), line], partner)
    c_z.wait_recv()
    c_pair2 = copy(cotbuf.at[pl.ds(2, 2), own], cotbuf.at[pl.ds(2, 2), own], partner)
    c_edge2 = copy(cotbuf.at[pl.ds(2, 2), 1 + 3 * core],
                   cotbuf.at[pl.ds(2, 2), 5 * (1 - core)], outer)

    third = []
    for h in range(2):
        for f in second[h]:
            f.wait_recv()
        p2, plus2, minus2 = places[h][3:]
        for a in range(3):
            parts = [wy[h, j, a].astype(F32)[0:12] for j in range(4)]
            wx[h, p2, a] = jnp.concatenate(parts, axis=0).astype(BF)
        third.append(gather_start(wx.at[h], p2, plus2, minus2))

    c_edge2.wait_recv()
    c_edge2_f = copy(cotbuf.at[pl.ds(2, 2), line], cotbuf.at[pl.ds(2, 2), line], partner)

    tot1 = stats_end(0, tot1, s1)
    mean_l = tot1[0:2] / n_norm
    inv_l = lax.rsqrt(tot1[2:4] / n_norm - mean_l * mean_l + NORM_EPS)
    wide = lambda m: jnp.concatenate(
        [jnp.broadcast_to(spread(m[t:t + 1]), (192, 128)) for t in range(2)], axis=1)
    inv = wide(inv_l)
    normed = (xt - wide(mean_l)) * inv
    shifted = normed * gcol + bcol
    gate = jax.nn.sigmoid(shifted)
    hidden = (shifted * gate).astype(BF)
    slope = gate * (1.0 + shifted * (1.0 - gate)) * gcol
    r2 = rows_iota((192, 192), 0)
    c2 = rows_iota((192, 192), 1)
    b2 = div12(r2)
    swap = c2 == r2 + 12 * ((b2 & 3) * 4 + (b2 >> 2) - b2)
    swap_bf = jnp.where(swap, 1.0, 0.0).astype(BF)
    hidden_b = jnp.dot(swap_bf, hidden, preferred_element_type=F32).astype(BF)
    hid = (hidden, hidden_b)

    c_pair.wait_recv()
    c_edge_f.wait_recv()
    c_pair2.wait_recv()
    c_edge2_f.wait_recv()
    left = rows_iota((64, 128), 1) < 64
    zero_row = jnp.zeros((1, 128), F32)

    def up(v):
        return jnp.concatenate([v[1:], zero_row], axis=0)

    def down(v):
        return jnp.concatenate([zero_row, v[:-1]], axis=0)

    def put(rows, lane, v):
        hi = v.astype(BF)
        ghi[rows, pl.ds(lane, 128)] = hi
        glo[rows, pl.ds(lane, 128)] = (v - hi.astype(F32)).astype(BF)

    for f in range(4):
        lines = []
        for h in range(6):
            v = cotbuf[f, h].astype(F32)
            if h == 0:
                v = jnp.where(q > 0, v, 0.0)
            if h == 5:
                v = jnp.where(q < 15, v, 0.0)
            if f >= 2:
                v = jnp.where(z < 7, v, 0.0)
            lines.append(v)
        for r in range(2):
            rows = pl.ds(f * 128 + r * 64, 64)
            tops = []
            for b in range(3):
                s = lines[2 * r + 2 - b] + lines[2 * r + 3 - b]
                even, odd, both = s[:, 0:128], s[:, 128:256], s[:, 256:384]
                other = pltpu.roll(both, 64, 1)
                even_t = jnp.where(left, both, other)
                odd_t = jnp.where(left, other, both)
                put(rows, (3 * b) * 128, odd + up(even))
                put(rows, (3 * b + 1) * 128, even + odd)
                put(rows, (3 * b + 2) * 128, down(odd) + even)
                tops += [odd_t + up(even_t), even_t + odd_t, down(odd_t) + even_t]
            for m in range(4):
                put(rows, 1152 + 128 * m, jnp.where(left, tops[2 * m], tops[2 * m + 1]))
            put(rows, 1664, jnp.where(left, tops[8], 0.0))

    def reduce_start(part, sbuf, p, plus, minus, r1, r2_, a_in, b_in):
        opp, nxt, prv = lax.rem(p + 2, 4), lax.rem(p + 1, 4), lax.rem(p + 3, 4)
        lo, hi = pl.ds(0, CUT), pl.ds(CUT, HALF - CUT)
        sbuf[opp] = part[opp].astype(BF)
        o1 = copy(sbuf.at[opp, :, :, lo], r1, plus)
        o2 = copy(sbuf.at[opp, :, :, hi], r2_, minus)
        sbuf[nxt] = part[nxt].astype(BF)
        n1 = copy(sbuf.at[nxt, :, :, hi], a_in.at[:, :, hi], plus)
        sbuf[prv] = part[prv].astype(BF)
        n2 = copy(sbuf.at[prv, :, :, lo], b_in.at[:, :, lo], minus)
        return o1, o2, n1, n2

    def reduce_mid(part, p, plus, minus, r1, r2_, a_in, b_in, s1_, s2_, cs):
        nxt, prv = lax.rem(p + 1, 4), lax.rem(p + 3, 4)
        lo, hi = pl.ds(0, CUT), pl.ds(CUT, HALF - CUT)
        cs[0].wait_recv()
        s1_[...] = (part[nxt, :, :, lo] + r1[...].astype(F32)).astype(BF)
        m1 = copy(s1_, a_in.at[:, :, lo], plus)
        cs[1].wait_recv()
        s2_[...] = (part[prv, :, :, hi] + r2_[...].astype(F32)).astype(BF)
        m2 = copy(s2_, b_in.at[:, :, hi], minus)
        return m1, m2

    def reduce_end(part, p, a_in, b_in, cs, ms):
        for c in (cs[2], cs[3], ms[0], ms[1]):
            c.wait_recv()
        return part[p] + a_in[...].astype(F32) + b_in[...].astype(F32)

    rs_places = (places[1], places[0])
    started = []
    for h in range(2):
        for a in range(3):
            rows, lanes = pl.ds((2 - a) * 128, 256), pl.ds(h * HALF, HALF)
            d = jnp.dot(hid[h], ghi[rows, lanes], preferred_element_type=F32)
            d = d + jnp.dot(hid[h], glo[rows, lanes], preferred_element_type=F32)
            for j in range(4):
                dpart[h, j, a] = d[48 * j:48 * j + 48]
        p, plus, minus = rs_places[h][:3]
        started.append(reduce_start(dpart.at[h], sb.at[h], p, plus, minus,
                                    rp1.at[h], rp2.at[h], ra.at[h], rb.at[h]))

    fourth = [gather_forward(wx.at[h], *places[h][3:], third[h]) for h in range(2)]

    mids = []
    for h in range(2):
        p, plus, minus = rs_places[h][:3]
        mids.append(reduce_mid(dpart.at[h], p, plus, minus, rp1.at[h], rp2.at[h], ra.at[h],
                               rb.at[h], sm1.at[h], sm2.at[h], started[h]))

    ag = []
    for h in range(2):
        for f in fourth[h]:
            f.wait_recv()
        acc = jnp.zeros((192, 256), F32)
        for a in range(3):
            rows, lanes = pl.ds((2 - a) * 128, 256), pl.ds(h * HALF, HALF)
            wa = jnp.concatenate([wx[h, j, a] for j in range(4)], axis=0)
            for g in (ghi, glo):
                acc = acc + lax.dot_general(wa, g[rows, lanes], (((1,), (1,)), ((), ())),
                                            preferred_element_type=F32)
        ag.append(acc)
    for m in range(16):
        perm_scr[12 * m:12 * m + 12, :] = ag[1][12 * ((m % 4) * 4 + m // 4):12 * ((m % 4) * 4 + m // 4) + 12]
    norm_grad = (ag[0] + perm_scr[...]) * slope
    tot2 = group_sums(norm_grad, norm_grad * normed)
    s2 = stats_start(1, tot2)

    second_rs = []
    for h in range(2):
        p = rs_places[h][0]
        whole = reduce_end(dpart.at[h], p, ra.at[h], rb.at[h], started[h], mids[h])
        for j in range(4):
            dpart2[h, j, :, 8:16] = jnp.zeros((3, 8, HALF), F32)
            for a in range(3):
                dpart2[h, j, a, 0:12] = whole[a, 12 * j:12 * j + 12]
        p2, plus2, minus2 = rs_places[h][3:]
        second_rs.append(reduce_start(dpart2.at[h], sb2.at[h], p2, plus2, minus2,
                                      rq1.at[h], rq2.at[h], ra2.at[h], rb2.at[h]))
    mids2 = []
    for h in range(2):
        p2, plus2, minus2 = rs_places[h][3:]
        mids2.append(reduce_mid(dpart2.at[h], p2, plus2, minus2, rq1.at[h], rq2.at[h], ra2.at[h],
                                rb2.at[h], sn1.at[h], sn2.at[h], second_rs[h]))

    tot2 = stats_end(1, tot2, s2)
    mean2 = tot2[0:4] / n_norm
    d = inv * (norm_grad - wide(mean2[0:2]) - normed * wide(mean2[2:4]))
    back = lax.dot_general(d.astype(BF), pick_bf, (((0,), (0,)), ((), ())),
                           preferred_element_type=F32)
    dsend[...] = back.astype(BF).reshape(2, 2, 64, 384)
    c_out = copy(dsend.at[:, 1 - core], drecv, partner)

    fin[42:48] = jnp.zeros((6, 16, 128), F32)
    for h in range(2):
        p2 = rs_places[h][3]
        done = reduce_end(dpart2.at[h], p2, ra2.at[h], rb2.at[h], second_rs[h], mids2[h])
        for a in range(3):
            for k in range(7):
                fin[h * 21 + a * 7 + k] = done[a, :, 128 * k:128 * k + 128]

    zs = []
    for k in range(1, 8):
        owner = lax.rem(z + k, 8)
        zs.append(copy(fin.at[pl.ds(6 * owner, 6)], zin.at[k - 1], column[k - 1]))
    c_out.wait_recv()
    dacts[...] = dsend[:, core] + drecv[...]
    total = fin[pl.ds(6 * z, 6)]
    for k in range(7):
        zs[k].wait_recv()
        total = total + zin[k]
    zred[...] = total
    zg = [copy(zred, zout.at[pl.ds(6 * z, 6)], column[k]) for k in range(7)]
    zout[pl.ds(6 * z, 6)] = total
    for c in zg:
        c.wait_recv()
    dw[...] = zout[0:42]
    for c in copies:
        c.wait_send()


def shards(acts, gamma, beta, weights, cotangent):
    frames, low_rows, low_cols, channels = acts.shape
    n_norm = float(low_rows * 32 * low_cols * (channels // GROUPS))
    acts2 = acts.reshape(2, 64, 384)
    pairs = cotangent.reshape(2, 2, 64, 2, 192)
    cot = jnp.concatenate(
        [pairs[..., 0, :128], pairs[..., 1, :128], pairs[..., 0, 128:], pairs[..., 1, 128:]], -1)
    w9 = weights.reshape(12, 3, 9, 192)
    w = jnp.concatenate(
        [w9[..., :128].reshape(12, 3, 1152), w9[..., 128:].reshape(12, 3, 576),
         jnp.zeros((12, 3, 64), BF)], -1)
    w = jnp.pad(w.reshape(12, 3, 2, HALF).transpose(2, 1, 0, 3), ((0, 0), (0, 0), (0, 4), (0, 0)))
    vm = pl.BlockSpec(memory_space=VMEM)
    dma = pltpu.SemaphoreType.DMA((NCOPY,))
    dacts, dw = pl.pallas_call(
        lambda *refs: kernel(n_norm, *refs),
        out_shape=(jax.ShapeDtypeStruct((2, 64, 384), BF),
                   jax.ShapeDtypeStruct((42, 16, 128), F32)),
        in_specs=[vm] * 5,
        out_specs=(vm, vm),
        scratch_shapes=[
            VMEM((2, 2, 64, 384), BF), VMEM((4, 6, 64, 384), BF),
            VMEM((2, 8, 128), F32), VMEM((2, 15, 8, 128), F32),
            VMEM((512, 1792), BF), VMEM((512, 1792), BF),
            VMEM((2, 4, 3, 16, HALF), BF), VMEM((2, 4, 3, 48, HALF), BF),
            VMEM((2, 4, 3, 48, HALF), F32), VMEM((2, 4, 3, 48, HALF), BF),
            VMEM((2, 3, 48, CUT), BF), VMEM((2, 3, 48, HALF - CUT), BF),
            VMEM((2, 3, 48, HALF), BF), VMEM((2, 3, 48, HALF), BF),
            VMEM((2, 3, 48, CUT), BF), VMEM((2, 3, 48, HALF - CUT), BF),
            VMEM((2, 4, 3, 16, HALF), F32), VMEM((2, 4, 3, 16, HALF), BF),
            VMEM((2, 3, 16, CUT), BF), VMEM((2, 3, 16, HALF - CUT), BF),
            VMEM((2, 3, 16, HALF), BF), VMEM((2, 3, 16, HALF), BF),
            VMEM((2, 3, 16, CUT), BF), VMEM((2, 3, 16, HALF - CUT), BF),
            VMEM((48, 16, 128), F32), VMEM((8, 128), F32), VMEM((7, 6, 16, 128), F32),
            VMEM((6, 16, 128), F32), VMEM((48, 16, 128), F32),
            VMEM((2, 2, 64, 384), BF), VMEM((2, 64, 384), BF), VMEM((192, 256), F32),
            dma, dma,
        ],
        compiler_params=pltpu.CompilerParams(
            collective_id=0, has_side_effects=True, vmem_limit_bytes=60 * 1024 * 1024),
        name="backward",
    )(acts2, cot, w, gamma.reshape(1, 384), beta.reshape(1, 384))
    flat = dw.reshape(2, 3, 7, 16, 128)[:, :, :, :12].transpose(3, 1, 0, 2, 4).reshape(12, 3, 1792)
    low = flat[..., :1152].reshape(12, 3, 9, 128)
    high = flat[..., 1152:1728].reshape(12, 3, 9, 64)
    d_weights = jnp.concatenate([low, high], -1).reshape(12, 27, 192)
    return dacts.reshape(2, 1, 64, 384), d_weights


def solution(mesh):
    placed = (
        P("block", "tile", None, None),
        P(),
        P(),
        P("tile", None, None),
        P("block", "tile", None, None),
    )
    return jax.shard_map(
        shards,
        mesh=mesh,
        in_specs=placed,
        out_specs=(P("block", "tile", None, None), P("tile", None, None)),
        check_vma=False,
    )
```

```python
import jax
import jax.numpy as jnp
from jax import lax
from jax.experimental import pallas as pl
from jax.experimental.pallas import tpu as pltpu
from jax.sharding import PartitionSpec as P

GROUPS = 32
NORM_EPS = 1e-06
MESH = pl.DeviceIdType.MESH
BF = jnp.bfloat16
F32 = jnp.float32
VMEM = pltpu.VMEM
NCOPY = 110
TAPK = 896
LANES = (1408, 1280)
CUTS = (768, 640)
SEGMENTS = (((0, 0, 896, 0), (1, 0, 512, 896)), ((1, 512, 384, 0), (2, 0, 896, 384)))


def iota(shape, dim):
    return lax.broadcasted_iota(jnp.int32, shape, dim)


def div12(v):
    return (v * 5462) >> 16


def kernel(n_norm, acts, cot, w, gamma, beta, dacts, dw,
           actbuf, cotbuf, stat_out, stat_in, ghi, glo, hbuf, hswap,
           wy0, wy1, wx0, wx1, dp0, dp1, sb0, sb1,
           r10, r11, r20, r21, ra0, ra1, rb0, rb1, sm0, sm1, sn0, sn1,
           ep0, ep1, eb0, eb1, q10, q11, q20, q21, ea0, ea1, ec0, ec1, tm0, tm1, tn0, tn1,
           fin, zin, zred, zout, actp, actin, perm_scr, dsend, drecv, send_sem, recv_sem):
    z = lax.axis_index("block")
    tile = lax.axis_index("tile")
    core = lax.rem(tile, 2)
    q = lax.div(tile, 2)
    y = lax.rem(q, 4)
    x = lax.div(q, 4)
    u = lax.rem(z, 2)
    pair = lax.div(z, 2)
    wy, wx = (wy0, wy1), (wx0, wx1)

    def chip(cx, cy):
        return {"tile": (cx * 4 + cy) * 2 + core}

    partner = {"tile": tile + 1 - 2 * core}
    outer = {"tile": lax.rem(tile + 2 * core - 1 + 32, 32)}
    xp, xm = chip(lax.rem(x + 1, 4), y), chip(lax.rem(x + 3, 4), y)
    yp, ym = chip(x, lax.rem(y + 1, 4)), chip(x, lax.rem(y + 3, 4))
    plane = [{"tile": lax.rem(q + d, 16) * 2 + core} for d in range(1, 16)]
    column = [{"block": lax.rem(z + k, 8)} for k in range(1, 8)]
    twin = {"block": z + 1 - 2 * u}

    copies = []
    count = [0]

    def make(src, dst, device, slot=None):
        k = count[0]
        count[0] += 1
        return pltpu.make_async_remote_copy(
            src_ref=src, dst_ref=dst, send_sem=send_sem.at[k],
            recv_sem=recv_sem.at[k if slot is None else slot],
            device_id=device, device_id_type=MESH)

    def copy(src, dst, device):
        c = make(src, dst, device)
        copies.append(c)
        c.start()
        return c

    barrier = pltpu.get_barrier_semaphore()
    friends = plane + column + [partner, outer]
    for dev in friends:
        pl.semaphore_signal(barrier, inc=1, device_id=dev, device_id_type=MESH)
    pl.semaphore_wait(barrier, len(friends))

    own = pl.ds(1 + 2 * core, 2)
    mine, theirs, later = pl.ds(2 * u, 2), pl.ds(2 - 2 * u, 2), pl.ds(4, 2)
    half = pl.ds(pl.multiple_of(96 * u, 32), 96)
    other_half = pl.ds(pl.multiple_of(96 - 96 * u, 32), 96)
    line, there = 5 * core, 5 * (1 - core)
    c_act = copy(acts, actbuf.at[:, core], partner)
    c_twin = copy(cot.at[:, :, other_half], cotbuf.at[mine, own], twin)
    slot = count[0]
    c_next1 = make(cot.at[:, :, pl.ds(0, 96)], cotbuf.at[later, own], column[5], slot)
    c_next2 = make(cot.at[:, :, pl.ds(96, 96)], cotbuf.at[later, own], column[6], slot)

    @pl.when(u == 0)
    def _():
        c_next1.start()
        c_next2.start()

    c_pair = copy(cot.at[:, :, half], cotbuf.at[mine, own], partner)
    c_edge = copy(cot.at[:, core, half], cotbuf.at[mine, there], outer)

    places = ((y, yp, ym, x, xp, xm), (x, xp, xm, y, yp, ym))

    def gather_start(buf, p, plus, minus):
        return copy(buf.at[p], buf.at[p], plus), copy(buf.at[p], buf.at[p], minus)

    def gather_forward(h, buf, p, plus, minus, pair_):
        lo, hi = pl.ds(0, CUTS[h]), pl.ds(CUTS[h], LANES[h] - CUTS[h])
        pair_[0].wait_recv()
        low = lax.rem(p + 3, 4)
        f1 = copy(buf.at[low, :, lo], buf.at[low, :, lo], plus)
        pair_[1].wait_recv()
        high = lax.rem(p + 1, 4)
        f2 = copy(buf.at[high, :, hi], buf.at[high, :, hi], minus)
        return f1, f2

    first = []
    for h in range(2):
        p, plus, minus = places[h][:3]
        wy[h][p] = w[u, :, 1408 * h:1408 * h + LANES[h]]
        first.append(gather_start(wy[h], p, plus, minus))

    actbuf[:, core] = acts[...]
    cotbuf[mine, own] = cot[:, :, half, :]
    blk = div12(iota((192, 384), 0))
    pick = iota((192, 384), 1) == iota((192, 384), 0) + 12 * blk + 12 * core
    pick_bf = jnp.where(pick, 1.0, 0.0).astype(BF)
    gcol = jnp.sum(jnp.where(pick, gamma[...][None, :], 0.0), axis=1, keepdims=True)
    bcol = jnp.sum(jnp.where(pick, beta[...][None, :], 0.0), axis=1, keepdims=True)
    member = iota((192, 128), 1) == div12(iota((192, 128), 0))
    c_act.wait_recv()
    xt = lax.dot_general(pick_bf, actbuf[...].reshape(256, 384), (((1,), (1,)), ((), ())),
                         preferred_element_type=F32)

    def group_sums(a, b):
        lines = []
        for value in (a, b):
            for t in range(2):
                c = jnp.sum(value[:, 128 * t:128 * t + 128], axis=1, keepdims=True)
                lines.append(jnp.sum(jnp.where(member, c, 0.0), axis=0, keepdims=True))
        return jnp.concatenate(lines + [jnp.zeros((4, 128), F32)], axis=0)

    def spread(v):
        return jnp.sum(jnp.where(member, v, 0.0), axis=1, keepdims=True)

    def stats_start(k, total):
        stat_out[k] = total
        return [copy(stat_out.at[k], stat_in.at[k, d], plane[d]) for d in range(15)]

    def stats_end(k, total, cs):
        for d in range(15):
            cs[d].wait_recv()
            total = total + stat_in[k, d]
        return total

    tot1 = group_sums(xt, xt * xt)
    s1 = stats_start(0, tot1)

    def pass_edge(frames, c):
        c.wait_recv()
        return copy(cotbuf.at[frames, line], cotbuf.at[frames, line], partner)

    def pass_rows(frames):
        return (copy(cotbuf.at[frames, own], cotbuf.at[frames, own], partner),
                copy(cotbuf.at[frames, 1 + 3 * core], cotbuf.at[frames, there], outer))

    cot_waits = [c_pair]
    second = [gather_forward(h, wy[h], *places[h][:3], first[h]) for h in range(2)]
    cot_waits.append(pass_edge(mine, c_edge))
    c_twin.wait_recv()
    rows1, edge1 = pass_rows(theirs)
    c_next1.wait_recv()
    rows2, edge2 = pass_rows(later)

    third = []
    for h in range(2):
        for f in second[h]:
            f.wait_recv()
        p2, plus2, minus2 = places[h][3:]
        parts = [wy[h][j].astype(F32)[0:12] for j in range(4)]
        wx[h][p2] = jnp.concatenate(parts, axis=0).astype(BF)
        third.append(gather_start(wx[h], p2, plus2, minus2))

    tot1 = stats_end(0, tot1, s1)
    mean_l = tot1[0:2] / n_norm
    inv_l = lax.rsqrt(tot1[2:4] / n_norm - mean_l * mean_l + NORM_EPS)
    wide = lambda m: jnp.concatenate(
        [jnp.broadcast_to(spread(m[t:t + 1]), (192, 128)) for t in range(2)], axis=1)
    inv = wide(inv_l)
    normed = (xt - wide(mean_l)) * inv
    shifted = normed * gcol + bcol
    gate = jax.nn.sigmoid(shifted)
    hidden = (shifted * gate).astype(BF)
    hbuf[u] = hidden
    c_hid = copy(hbuf.at[u], hbuf.at[u], twin)
    slope = gate * (1.0 + shifted * (1.0 - gate)) * gcol
    b2 = div12(iota((192, 192), 0))
    swap = iota((192, 192), 1) == iota((192, 192), 0) + 12 * ((b2 & 3) * 4 + (b2 >> 2) - b2)
    swap_bf = jnp.where(swap, 1.0, 0.0).astype(BF)
    hswap[u] = jnp.dot(swap_bf, hidden, preferred_element_type=F32).astype(BF)

    cot_waits.append(pass_edge(theirs, edge1))
    cot_waits.append(pass_edge(later, edge2))
    for c in cot_waits + [rows1, rows2]:
        c.wait_recv()
    left = iota((96, 128), 1) < 64
    col, lane = iota((128, 384), 0), iota((128, 384), 1)
    shift = col - 2 * (lane & 63) + (lane >> 7) - 1
    summer = jnp.where((shift == 0) | (shift == 1), 1.0, 0.0).astype(BF)
    ghi[864:896] = jnp.zeros((32, 768), BF)
    glo[864:896] = jnp.zeros((32, 768), BF)
    for f in range(6):
        sums = jnp.dot(cotbuf[f].reshape(576, 128), summer, preferred_element_type=F32)
        if f >= 4:
            sums = jnp.where(pair < 3, sums, 0.0)
        lines = [sums[96 * h:96 * h + 96] for h in range(6)]
        lines[0] = jnp.where(q > 0, lines[0], 0.0)
        lines[5] = jnp.where(q < 15, lines[5], 0.0)
        for e in range(3):
            ls = [v[:, 128 * e:128 * e + 128] for v in lines]
            for b in range(3):
                v = jnp.where(left, ls[2 - b] + ls[3 - b], ls[4 - b] + ls[5 - b])
                hi = v.astype(BF)
                k = (3 * b + e) * 96
                ghi[k:k + 96, 128 * f:128 * f + 128] = hi
                glo[k:k + 96, 128 * f:128 * f + 128] = (v - hi.astype(F32)).astype(BF)

    fourth = [gather_forward(h, wx[h], *places[h][3:], third[h]) for h in range(2)]

    def reduce_start(h, part, sbuf, p, plus, minus, r1, r2, a_in, b_in):
        opp, nxt, prv = lax.rem(p + 2, 4), lax.rem(p + 1, 4), lax.rem(p + 3, 4)
        lo, hi = pl.ds(0, CUTS[h]), pl.ds(CUTS[h], LANES[h] - CUTS[h])
        sbuf[opp] = part[opp].astype(BF)
        o1 = copy(sbuf.at[opp, :, lo], r1, plus)
        o2 = copy(sbuf.at[opp, :, hi], r2, minus)
        sbuf[nxt] = part[nxt].astype(BF)
        n1 = copy(sbuf.at[nxt, :, hi], a_in.at[:, hi], plus)
        sbuf[prv] = part[prv].astype(BF)
        n2 = copy(sbuf.at[prv, :, lo], b_in.at[:, lo], minus)
        return o1, o2, n1, n2

    def reduce_mid(h, part, p, plus, minus, r1, r2, a_in, b_in, s_1, s_2, cs):
        nxt, prv = lax.rem(p + 1, 4), lax.rem(p + 3, 4)
        lo, hi = pl.ds(0, CUTS[h]), pl.ds(CUTS[h], LANES[h] - CUTS[h])
        cs[0].wait_recv()
        s_1[...] = (part[nxt, :, lo] + r1[...].astype(F32)).astype(BF)
        m1 = copy(s_1, a_in.at[:, lo], plus)
        cs[1].wait_recv()
        s_2[...] = (part[prv, :, hi] + r2[...].astype(F32)).astype(BF)
        m2 = copy(s_2, b_in.at[:, hi], minus)
        return m1, m2

    def reduce_end(part, p, a_in, b_in, cs, ms):
        for c in (cs[2], cs[3], ms[0], ms[1]):
            c.wait_recv()
        return part[p] + a_in[...].astype(F32) + b_in[...].astype(F32)

    rs_places = (places[1], places[0])
    hid = (hbuf, hswap)
    dp, sb = (dp0, dp1), (sb0, sb1)
    rs_in = ((r10, r20, ra0, rb0), (r11, r21, ra1, rb1))
    rs_mid = ((sm0, sn0), (sm1, sn1))

    def partial(h, v):
        outs = []
        for a, k0, rows, _ in SEGMENTS[h]:
            lanes = pl.ds(pl.multiple_of(256 * v + (2 - a) * 128, 128), 256)
            acc = None
            for g in (ghi, glo):
                d = lax.dot_general(hid[h][v], g[k0:k0 + rows, lanes], (((1,), (1,)), ((), ())),
                                    preferred_element_type=F32)
                acc = d if acc is None else acc + d
            outs.append(acc)
        return outs

    for h in range(2):
        for (a, k0, rows, l0), d in zip(SEGMENTS[h], partial(h, u)):
            for j in range(4):
                dp[h][j, :, l0:l0 + rows] = d[48 * j:48 * j + 48]
    c_hid.wait_recv()
    hswap[1 - u] = jnp.dot(swap_bf, hbuf[1 - u], preferred_element_type=F32).astype(BF)
    started = []
    for h in range(2):
        for (a, k0, rows, l0), d in zip(SEGMENTS[h], partial(h, 1 - u)):
            for j in range(4):
                dp[h][j, :, l0:l0 + rows] += d[48 * j:48 * j + 48]
        p, plus, minus = rs_places[h][:3]
        started.append(reduce_start(h, dp[h], sb[h], p, plus, minus, *rs_in[h]))

    ag = []
    for h in range(2):
        for f in fourth[h]:
            f.wait_recv()
        acc = jnp.zeros((192, 512), F32)
        for a, k0, rows, l0 in SEGMENTS[h]:
            wa = jnp.concatenate([wx[h][j, :, l0:l0 + rows] for j in range(4)], axis=0)
            for g in (ghi, glo):
                acc = acc + jnp.dot(wa, g[k0:k0 + rows, (2 - a) * 128:(2 - a) * 128 + 512],
                                    preferred_element_type=F32)
        ag.append(acc)
    for m in range(16):
        b = (m % 4) * 4 + m // 4
        perm_scr[12 * m:12 * m + 12, :] = ag[1][12 * b:12 * b + 12]
    for v in range(2):
        actp[v] = ag[0][:, 256 * v:256 * v + 256] + perm_scr[:, 256 * v:256 * v + 256]
    c_grad = copy(actp.at[1 - u], actin, twin)

    mids = []
    for h in range(2):
        p, plus, minus = rs_places[h][:3]
        mids.append(reduce_mid(h, dp[h], p, plus, minus, *rs_in[h], *rs_mid[h], started[h]))

    c_grad.wait_recv()
    norm_grad = (actp[u] + actin[...]) * slope
    tot2 = group_sums(norm_grad, norm_grad * normed)
    s2 = stats_start(1, tot2)

    ep, eb = (ep0, ep1), (eb0, eb1)
    rs_in2 = ((q10, q20, ea0, ec0), (q11, q21, ea1, ec1))
    rs_mid2 = ((tm0, tn0), (tm1, tn1))
    second_rs = []
    for h in range(2):
        p = rs_places[h][0]
        whole = reduce_end(dp[h], p, rs_in[h][2], rs_in[h][3], started[h], mids[h])
        for j in range(4):
            ep[h][j, 8:16] = jnp.zeros((8, LANES[h]), F32)
            ep[h][j, 0:12] = whole[12 * j:12 * j + 12]
        p2, plus2, minus2 = rs_places[h][3:]
        second_rs.append(reduce_start(h, ep[h], eb[h], p2, plus2, minus2, *rs_in2[h]))
    mids2 = []
    for h in range(2):
        p2, plus2, minus2 = rs_places[h][3:]
        mids2.append(reduce_mid(h, ep[h], p2, plus2, minus2, *rs_in2[h], *rs_mid2[h],
                                second_rs[h]))

    tot2 = stats_end(1, tot2, s2)
    mean2 = tot2[0:4] / n_norm
    d = inv * (norm_grad - wide(mean2[0:2]) - normed * wide(mean2[2:4]))
    back = lax.dot_general(d.astype(BF), pick_bf, (((0,), (0,)), ((), ())),
                           preferred_element_type=F32)
    dsend[...] = back.astype(BF).reshape(2, 2, 64, 384)
    c_out = copy(dsend.at[:, 1 - core], drecv, partner)

    rest = []
    for h in range(2):
        p2 = rs_places[h][3]
        done = reduce_end(ep[h], p2, rs_in2[h][2], rs_in2[h][3], second_rs[h], mids2[h])
        for k in range(LANES[h] // 128):
            fin[11 * h + k] = done[0:8, 128 * k:128 * k + 128]
            rest.append(done[8:12, 128 * k:128 * k + 128])
    rest.append(jnp.zeros((4, 128), F32))
    for m in range(11):
        fin[21 + m] = jnp.concatenate([rest[2 * m], rest[2 * m + 1]], axis=0)

    zs = []
    for m in range(1, 4):
        owner = lax.rem(pair + m, 4)
        zs.append(copy(fin.at[pl.ds(8 * owner, 8)], zin.at[m - 1], column[2 * m - 1]))
    c_out.wait_recv()
    dacts[...] = dsend[:, core] + drecv[...]
    total = fin[pl.ds(8 * pair, 8)]
    for m in range(3):
        zs[m].wait_recv()
        total = total + zin[m]
    zred[...] = total
    zg = [copy(zred, zout.at[u, pl.ds(8 * pair, 8)], column[k]) for k in range(7)]
    zout[u, pl.ds(8 * pair, 8)] = total
    for c in zg:
        c.wait_recv()
    dw[...] = zout[...]
    for c in copies:
        c.wait_send()

    @pl.when(u == 0)
    def _():
        c_next1.wait_send()
        c_next2.wait_send()


def shards(acts, gamma, beta, weights, cotangent):
    frames, low_rows, low_cols, channels = acts.shape
    n_norm = float(low_rows * 32 * low_cols * (channels // GROUPS))
    acts2 = acts.reshape(2, 64, 384)
    cot = cotangent.swapaxes(2, 3)
    w = weights.reshape(12, 3, 9, 2, 96).transpose(3, 0, 1, 2, 4).reshape(2, 12, 3, 864)
    w = jnp.pad(w, ((0, 0), (0, 4), (0, 0), (0, 32))).reshape(2, 16, 3 * TAPK)
    vm = pl.BlockSpec(memory_space=VMEM)
    dma = pltpu.SemaphoreType.DMA((NCOPY,))
    both = lambda lead, dtype, lanes=LANES: [VMEM((*lead, n), dtype) for n in lanes]
    tails = tuple(n - c for n, c in zip(LANES, CUTS))

    def ring(rows):
        return (both((4, rows), F32) + both((4, rows), BF) + both((rows,), BF, CUTS)
                + both((rows,), BF, tails) + both((rows,), BF) + both((rows,), BF)
                + both((rows,), BF, CUTS) + both((rows,), BF, tails))

    dacts, dw = pl.pallas_call(
        lambda *refs: kernel(n_norm, *refs),
        out_shape=(jax.ShapeDtypeStruct((2, 64, 384), BF),
                   jax.ShapeDtypeStruct((2, 32, 8, 128), F32)),
        in_specs=[vm] * 5,
        out_specs=(vm, vm),
        scratch_shapes=[
            VMEM((2, 2, 64, 384), BF), VMEM((6, 6, 96, 128), BF),
            VMEM((2, 8, 128), F32), VMEM((2, 15, 8, 128), F32),
            VMEM((TAPK, 768), BF), VMEM((TAPK, 768), BF),
            VMEM((2, 192, 256), BF), VMEM((2, 192, 256), BF),
            *both((4, 16), BF), *both((4, 48), BF), *ring(48), *ring(16),
            VMEM((32, 8, 128), F32), VMEM((3, 8, 8, 128), F32), VMEM((8, 8, 128), F32),
            VMEM((2, 32, 8, 128), F32),
            VMEM((2, 192, 256), F32), VMEM((192, 256), F32), VMEM((192, 512), F32),
            VMEM((2, 2, 64, 384), BF), VMEM((2, 64, 384), BF),
            dma, dma,
        ],
        compiler_params=pltpu.CompilerParams(
            collective_id=0, has_side_effects=True, vmem_limit_bytes=60 * 1024 * 1024),
        name="backward",
    )(acts2, cot, w, gamma, beta)
    top = dw[:, :21]
    rest = dw[:, 21:].reshape(2, 22, 4, 128)[:, :21]
    flat = jnp.concatenate([top, rest], 2).reshape(2, 3, 7, 12, 128)
    flat = flat.transpose(3, 1, 0, 2, 4).reshape(12, 3, 2, TAPK)[..., :864]
    d_weights = flat.reshape(12, 3, 2, 9, 96).transpose(0, 1, 3, 2, 4).reshape(12, 27, 192)
    return dacts.reshape(2, 1, 64, 384), d_weights


def solution(mesh):
    placed = (
        P("block", "tile", None, None),
        P(),
        P(),
        P("tile", None, None),
        P("block", "tile", None, None),
    )
    return jax.shard_map(
        shards,
        mesh=mesh,
        in_specs=placed,
        out_specs=(P("block", "tile", None, None), P("tile", None, None)),
        check_vma=False,
    )
```

```python
import jax
import jax.numpy as jnp
from jax import lax
from jax.experimental import pallas as pl
from jax.experimental.pallas import tpu as pltpu
from jax.sharding import PartitionSpec as P

GROUPS = 32
NORM_EPS = 1e-06
MESH = pl.DeviceIdType.MESH
BF = jnp.bfloat16
F32 = jnp.float32
VMEM = pltpu.VMEM
NCOPY = 110
TAPK = 896
LANES = (1408, 1280)
CUTS = (768, 640)
SEGMENTS = (((0, 0, 896, 0), (1, 0, 512, 896)), ((1, 512, 384, 0), (2, 0, 896, 384)))


def iota(shape, dim):
    return lax.broadcasted_iota(jnp.int32, shape, dim)


def div12(v):
    return (v * 5462) >> 16


def kernel(n_norm, acts, cot, w, gamma, beta, dacts, dw,
           actbuf, cotbuf, stat_out, stat_in, ghi, glo, hbuf, hswap, wflat, dflat,
           wy0, wy1, wx0, wx1, dp0, dp1, sb0, sb1,
           r10, r11, r20, r21, ra0, ra1, rb0, rb1, sm0, sm1, sn0, sn1,
           ep0, ep1, eb0, eb1, q10, q11, q20, q21, ea0, ea1, ec0, ec1, tm0, tm1, tn0, tn1,
           fin, zin, zred, zout, actp, actin, perm_scr, dsend, drecv, send_sem, recv_sem):
    z = lax.axis_index("block")
    tile = lax.axis_index("tile")
    core = lax.rem(tile, 2)
    q = lax.div(tile, 2)
    y = lax.rem(q, 4)
    x = lax.div(q, 4)
    u = lax.rem(z, 2)
    pair = lax.div(z, 2)
    wy, wx = (wy0, wy1), (wx0, wx1)

    def chip(cx, cy):
        return {"tile": (cx * 4 + cy) * 2 + core}

    partner = {"tile": tile + 1 - 2 * core}
    outer = {"tile": lax.rem(tile + 2 * core - 1 + 32, 32)}
    xp, xm = chip(lax.rem(x + 1, 4), y), chip(lax.rem(x + 3, 4), y)
    yp, ym = chip(x, lax.rem(y + 1, 4)), chip(x, lax.rem(y + 3, 4))
    plane = [{"tile": lax.rem(q + d, 16) * 2 + core} for d in range(1, 16)]
    column = [{"block": lax.rem(z + k, 8)} for k in range(1, 8)]
    twin = {"block": z + 1 - 2 * u}

    copies = []
    count = [0]

    def make(src, dst, device, slot=None):
        k = count[0]
        count[0] += 1
        return pltpu.make_async_remote_copy(
            src_ref=src, dst_ref=dst, send_sem=send_sem.at[k],
            recv_sem=recv_sem.at[k if slot is None else slot],
            device_id=device, device_id_type=MESH)

    def copy(src, dst, device):
        c = make(src, dst, device)
        copies.append(c)
        c.start()
        return c

    barrier = pltpu.get_barrier_semaphore()
    friends = plane + column + [partner, outer]
    for dev in friends:
        pl.semaphore_signal(barrier, inc=1, device_id=dev, device_id_type=MESH)
    pl.semaphore_wait(barrier, len(friends))

    own = pl.ds(1 + 2 * core, 2)
    mine, theirs, later = pl.ds(2 * u, 2), pl.ds(2 - 2 * u, 2), pl.ds(4, 2)
    half = pl.ds(pl.multiple_of(96 * u, 32), 96)
    other_half = pl.ds(pl.multiple_of(96 - 96 * u, 32), 96)
    line, there = 5 * core, 5 * (1 - core)
    c_act = copy(acts, actbuf.at[:, core], partner)
    edge_row, inner_row = 1 + 3 * core, 2 + core
    nexts, c_twin, c_next = [], [], []
    for r, dst_row in ((core, edge_row), (1 - core, inner_row)):
        slot = count[0]
        c_next.append(make(cot.at[:, r, pl.ds(0, 96)], cotbuf.at[later, dst_row], column[5], slot))
        nexts.append(c_next[-1])
        nexts.append(make(cot.at[:, r, pl.ds(96, 96)], cotbuf.at[later, dst_row], column[6], slot))

        @pl.when(u == 0)
        def _(pair_=nexts[-2:]):
            for c in pair_:
                c.start()

        c_twin.append(copy(cot.at[:, r, other_half], cotbuf.at[mine, dst_row], twin))

    c_pair = copy(cot.at[:, :, half], cotbuf.at[mine, own], partner)
    c_edge = copy(cot.at[:, core, half], cotbuf.at[mine, there], outer)

    places = ((y, yp, ym, x, xp, xm), (x, xp, xm, y, yp, ym))

    def gather_start(buf, p, plus, minus):
        return copy(buf.at[p], buf.at[p], plus), copy(buf.at[p], buf.at[p], minus)

    def gather_forward(h, buf, p, plus, minus, pair_):
        lo, hi = pl.ds(0, CUTS[h]), pl.ds(CUTS[h], LANES[h] - CUTS[h])
        pair_[0].wait_recv()
        low = lax.rem(p + 3, 4)
        f1 = copy(buf.at[low, :, lo], buf.at[low, :, lo], plus)
        pair_[1].wait_recv()
        high = lax.rem(p + 1, 4)
        f2 = copy(buf.at[high, :, hi], buf.at[high, :, hi], minus)
        return f1, f2

    first = []
    wide_w = w[...].astype(F32)
    wide_w = jnp.where(u == 0, wide_w[..., 0:96], wide_w[..., 96:192])
    for a in range(3):
        for b in range(9):
            k = a * TAPK + 96 * b
            wflat[0:12, k:k + 96] = wide_w[:, 9 * a + b, :]
        wflat[0:12, a * TAPK + 864:a * TAPK + TAPK] = jnp.zeros((12, 32), F32)
    for h in range(2):
        p, plus, minus = places[h][:3]
        wy[h][p] = wflat[:, 1408 * h:1408 * h + LANES[h]].astype(BF)
        first.append(gather_start(wy[h], p, plus, minus))

    actbuf[:, core] = acts[...]
    cotbuf[mine, own] = cot[:, :, half, :]
    blk = div12(iota((192, 384), 0))
    pick = iota((192, 384), 1) == iota((192, 384), 0) + 12 * blk + 12 * core
    pick_bf = jnp.where(pick, 1.0, 0.0).astype(BF)
    gcol = jnp.sum(jnp.where(pick, gamma[...][None, :], 0.0), axis=1, keepdims=True)
    bcol = jnp.sum(jnp.where(pick, beta[...][None, :], 0.0), axis=1, keepdims=True)
    member = iota((192, 128), 1) == div12(iota((192, 128), 0))
    c_act.wait_recv()
    xt = lax.dot_general(pick_bf, actbuf[...].reshape(256, 384), (((1,), (1,)), ((), ())),
                         preferred_element_type=F32)

    def group_sums(a, b):
        lines = []
        for value in (a, b):
            for t in range(2):
                c = jnp.sum(value[:, 128 * t:128 * t + 128], axis=1, keepdims=True)
                lines.append(jnp.sum(jnp.where(member, c, 0.0), axis=0, keepdims=True))
        return jnp.concatenate(lines + [jnp.zeros((4, 128), F32)], axis=0)

    def spread(v):
        return jnp.sum(jnp.where(member, v, 0.0), axis=1, keepdims=True)

    def stats_start(k, total):
        stat_out[k] = total
        return [copy(stat_out.at[k], stat_in.at[k, d], plane[d]) for d in range(15)]

    def stats_end(k, total, cs):
        for d in range(15):
            cs[d].wait_recv()
            total = total + stat_in[k, d]
        return total

    tot1 = group_sums(xt, xt * xt)
    s1 = stats_start(0, tot1)

    def pass_edge(frames, c):
        c.wait_recv()
        return copy(cotbuf.at[frames, line], cotbuf.at[frames, line], partner)

    def pass_row(frames, r, device, to, c):
        if c is not None:
            c.wait_recv()
        return copy(cotbuf.at[frames, r], cotbuf.at[frames, to], device)

    early, late = [c_pair], []
    second = [gather_forward(h, wy[h], *places[h][:3], first[h]) for h in range(2)]
    early.append(pass_edge(mine, c_edge))
    edge1 = pass_row(theirs, edge_row, outer, there, c_twin[0])
    early.append(pass_row(theirs, edge_row, partner, edge_row, None))
    edge2 = pass_row(later, edge_row, outer, there, c_next[0])
    late.append(pass_row(later, edge_row, partner, edge_row, None))
    early.append(pass_row(theirs, inner_row, partner, inner_row, c_twin[1]))

    tot1 = stats_end(0, tot1, s1)
    mean_l = tot1[0:2] / n_norm
    inv_l = lax.rsqrt(tot1[2:4] / n_norm - mean_l * mean_l + NORM_EPS)
    wide = lambda m: jnp.concatenate(
        [jnp.broadcast_to(spread(m[t:t + 1]), (192, 128)) for t in range(2)], axis=1)
    inv = wide(inv_l)
    normed = (xt - wide(mean_l)) * inv
    shifted = normed * gcol + bcol
    gate = jax.nn.sigmoid(shifted)
    hidden = (shifted * gate).astype(BF)
    hbuf[u] = hidden
    c_hid = copy(hbuf.at[u], hbuf.at[u], twin)
    slope = gate * (1.0 + shifted * (1.0 - gate)) * gcol
    b2 = div12(iota((192, 192), 0))
    swap = iota((192, 192), 1) == iota((192, 192), 0) + 12 * ((b2 & 3) * 4 + (b2 >> 2) - b2)
    swap_bf = jnp.where(swap, 1.0, 0.0).astype(BF)
    hswap[u] = jnp.dot(swap_bf, hidden, preferred_element_type=F32).astype(BF)

    third = []
    for h in range(2):
        for f in second[h]:
            f.wait_recv()
        p2, plus2, minus2 = places[h][3:]
        parts = [wy[h][j].astype(F32)[0:12] for j in range(4)]
        wx[h][p2] = jnp.concatenate(parts, axis=0).astype(BF)
        third.append(gather_start(wx[h], p2, plus2, minus2))

    early.append(pass_edge(theirs, edge1))
    late.append(pass_row(later, inner_row, partner, inner_row, c_next[1]))
    late.append(pass_edge(later, edge2))
    for c in early:
        c.wait_recv()
    left = iota((96, 128), 1) < 64
    col, lane = iota((128, 384), 0), iota((128, 384), 1)
    shift = col - 2 * (lane & 63) + (lane >> 7) - 1
    summer = jnp.where((shift == 0) | (shift == 1), 1.0, 0.0).astype(BF)
    ghi[864:896] = jnp.zeros((32, 768), BF)
    glo[864:896] = jnp.zeros((32, 768), BF)
    for f in range(6):
        if f == 4:
            for c in late:
                c.wait_recv()
        sums = jnp.dot(cotbuf[f].reshape(576, 128), summer, preferred_element_type=F32)
        if f >= 4:
            sums = jnp.where(pair < 3, sums, 0.0)
        lines = [sums[96 * h:96 * h + 96] for h in range(6)]
        lines[0] = jnp.where(q > 0, lines[0], 0.0)
        lines[5] = jnp.where(q < 15, lines[5], 0.0)
        for e in range(3):
            ls = [v[:, 128 * e:128 * e + 128] for v in lines]
            for b in range(3):
                v = jnp.where(left, ls[2 - b] + ls[3 - b], ls[4 - b] + ls[5 - b])
                hi = v.astype(BF)
                k = (3 * b + e) * 96
                ghi[k:k + 96, 128 * f:128 * f + 128] = hi
                glo[k:k + 96, 128 * f:128 * f + 128] = (v - hi.astype(F32)).astype(BF)

    fourth = [gather_forward(h, wx[h], *places[h][3:], third[h]) for h in range(2)]

    def reduce_start(h, part, sbuf, p, plus, minus, r1, r2, a_in, b_in):
        opp, nxt, prv = lax.rem(p + 2, 4), lax.rem(p + 1, 4), lax.rem(p + 3, 4)
        lo, hi = pl.ds(0, CUTS[h]), pl.ds(CUTS[h], LANES[h] - CUTS[h])
        sbuf[opp] = part[opp].astype(BF)
        o1 = copy(sbuf.at[opp, :, lo], r1, plus)
        o2 = copy(sbuf.at[opp, :, hi], r2, minus)
        sbuf[nxt] = part[nxt].astype(BF)
        n1 = copy(sbuf.at[nxt, :, hi], a_in.at[:, hi], plus)
        sbuf[prv] = part[prv].astype(BF)
        n2 = copy(sbuf.at[prv, :, lo], b_in.at[:, lo], minus)
        return o1, o2, n1, n2

    def reduce_mid(h, part, p, plus, minus, r1, r2, a_in, b_in, s_1, s_2, cs):
        nxt, prv = lax.rem(p + 1, 4), lax.rem(p + 3, 4)
        lo, hi = pl.ds(0, CUTS[h]), pl.ds(CUTS[h], LANES[h] - CUTS[h])
        cs[0].wait_recv()
        s_1[...] = (part[nxt, :, lo] + r1[...].astype(F32)).astype(BF)
        m1 = copy(s_1, a_in.at[:, lo], plus)
        cs[1].wait_recv()
        s_2[...] = (part[prv, :, hi] + r2[...].astype(F32)).astype(BF)
        m2 = copy(s_2, b_in.at[:, hi], minus)
        return m1, m2

    def reduce_end(part, p, a_in, b_in, cs, ms):
        for c in (cs[2], cs[3], ms[0], ms[1]):
            c.wait_recv()
        return part[p] + a_in[...].astype(F32) + b_in[...].astype(F32)

    rs_places = (places[1], places[0])
    hid = (hbuf, hswap)
    dp, sb = (dp0, dp1), (sb0, sb1)
    rs_in = ((r10, r20, ra0, rb0), (r11, r21, ra1, rb1))
    rs_mid = ((sm0, sn0), (sm1, sn1))

    def partial(h, v):
        outs = []
        for a, k0, rows, _ in SEGMENTS[h]:
            lanes = pl.ds(pl.multiple_of(256 * v + (2 - a) * 128, 128), 256)
            acc = None
            for g in (ghi, glo):
                d = lax.dot_general(hid[h][v], g[k0:k0 + rows, lanes], (((1,), (1,)), ((), ())),
                                    preferred_element_type=F32)
                acc = d if acc is None else acc + d
            outs.append(acc)
        return outs

    for h in range(2):
        for (a, k0, rows, l0), d in zip(SEGMENTS[h], partial(h, u)):
            for j in range(4):
                dp[h][j, :, l0:l0 + rows] = d[48 * j:48 * j + 48]
    c_hid.wait_recv()
    hswap[1 - u] = jnp.dot(swap_bf, hbuf[1 - u], preferred_element_type=F32).astype(BF)
    started = []
    for h in range(2):
        for (a, k0, rows, l0), d in zip(SEGMENTS[h], partial(h, 1 - u)):
            for j in range(4):
                dp[h][j, :, l0:l0 + rows] += d[48 * j:48 * j + 48]
        p, plus, minus = rs_places[h][:3]
        started.append(reduce_start(h, dp[h], sb[h], p, plus, minus, *rs_in[h]))

    ag = []
    for h in range(2):
        for f in fourth[h]:
            f.wait_recv()
        acc = jnp.zeros((192, 512), F32)
        for a, k0, rows, l0 in SEGMENTS[h]:
            wa = jnp.concatenate([wx[h][j, :, l0:l0 + rows] for j in range(4)], axis=0)
            for g in (ghi, glo):
                acc = acc + jnp.dot(wa, g[k0:k0 + rows, (2 - a) * 128:(2 - a) * 128 + 512],
                                    preferred_element_type=F32)
        ag.append(acc)
    for m in range(16):
        b = (m % 4) * 4 + m // 4
        perm_scr[12 * m:12 * m + 12, :] = ag[1][12 * b:12 * b + 12]
    for v in range(2):
        actp[v] = ag[0][:, 256 * v:256 * v + 256] + perm_scr[:, 256 * v:256 * v + 256]
    c_grad = copy(actp.at[1 - u], actin, twin)

    mids = []
    for h in range(2):
        p, plus, minus = rs_places[h][:3]
        mids.append(reduce_mid(h, dp[h], p, plus, minus, *rs_in[h], *rs_mid[h], started[h]))

    ep, eb = (ep0, ep1), (eb0, eb1)
    rs_in2 = ((q10, q20, ea0, ec0), (q11, q21, ea1, ec1))
    rs_mid2 = ((tm0, tn0), (tm1, tn1))
    second_rs = []
    for h in range(2):
        p = rs_places[h][0]
        whole = reduce_end(dp[h], p, rs_in[h][2], rs_in[h][3], started[h], mids[h])
        for j in range(4):
            ep[h][j, 8:16] = jnp.zeros((8, LANES[h]), F32)
            ep[h][j, 0:12] = whole[12 * j:12 * j + 12]
        p2, plus2, minus2 = rs_places[h][3:]
        second_rs.append(reduce_start(h, ep[h], eb[h], p2, plus2, minus2, *rs_in2[h]))
    c_grad.wait_recv()
    norm_grad = (actp[u] + actin[...]) * slope
    tot2 = group_sums(norm_grad, norm_grad * normed)
    s2 = stats_start(1, tot2)

    mids2 = []
    for h in range(2):
        p2, plus2, minus2 = rs_places[h][3:]
        mids2.append(reduce_mid(h, ep[h], p2, plus2, minus2, *rs_in2[h], *rs_mid2[h],
                                second_rs[h]))

    tot2 = stats_end(1, tot2, s2)
    mean2 = tot2[0:4] / n_norm
    d = inv * (norm_grad - wide(mean2[0:2]) - normed * wide(mean2[2:4]))
    back = lax.dot_general(d.astype(BF), pick_bf, (((0,), (0,)), ((), ())),
                           preferred_element_type=F32)
    dsend[...] = back.astype(BF).reshape(2, 2, 64, 384)
    c_out = copy(dsend.at[:, 1 - core], drecv, partner)

    rest = []
    for h in range(2):
        p2 = rs_places[h][3]
        done = reduce_end(ep[h], p2, rs_in2[h][2], rs_in2[h][3], second_rs[h], mids2[h])
        for k in range(LANES[h] // 128):
            fin[11 * h + k] = done[0:8, 128 * k:128 * k + 128]
            rest.append(done[8:12, 128 * k:128 * k + 128])
    rest.append(jnp.zeros((4, 128), F32))
    for m in range(11):
        fin[21 + m] = jnp.concatenate([rest[2 * m], rest[2 * m + 1]], axis=0)

    zs = []
    for m in range(1, 4):
        owner = lax.rem(pair + m, 4)
        zs.append(copy(fin.at[pl.ds(8 * owner, 8)], zin.at[m - 1], column[2 * m - 1]))
    c_out.wait_recv()
    dacts[...] = dsend[:, core] + drecv[...]
    total = fin[pl.ds(8 * pair, 8)]
    for m in range(3):
        zs[m].wait_recv()
        total = total + zin[m]
    zred[...] = total
    zg = [copy(zred, zout.at[u, pl.ds(8 * pair, 8)], column[k]) for k in range(7)]
    zout[u, pl.ds(8 * pair, 8)] = total
    for c in zg:
        c.wait_recv()
    for v in range(2):
        for k in range(21):
            dflat[v, 0:8, 128 * k:128 * k + 128] = zout[v, k]
        for m in range(11):
            two = zout[v, 21 + m]
            dflat[v, 8:12, 256 * m:256 * m + 128] = two[0:4]
            if m < 10:
                dflat[v, 8:12, 256 * m + 128:256 * m + 256] = two[4:8]
    for a in range(3):
        for b in range(9):
            k = a * TAPK + 96 * b
            dw[:, 9 * a + b, 0:96] = dflat[0, 0:12, k:k + 96]
            dw[:, 9 * a + b, 96:192] = dflat[1, 0:12, k:k + 96]
    for c in copies:
        c.wait_send()

    @pl.when(u == 0)
    def _():
        for c in nexts:
            c.wait_send()


def shards(acts, gamma, beta, weights, cotangent):
    frames, low_rows, low_cols, channels = acts.shape
    n_norm = float(low_rows * 32 * low_cols * (channels // GROUPS))
    acts2 = acts.reshape(2, 64, 384)
    cot = cotangent.swapaxes(2, 3)
    vm = pl.BlockSpec(memory_space=VMEM)
    dma = pltpu.SemaphoreType.DMA((NCOPY,))
    both = lambda lead, dtype, lanes=LANES: [VMEM((*lead, n), dtype) for n in lanes]
    tails = tuple(n - c for n, c in zip(LANES, CUTS))

    def ring(rows):
        return (both((4, rows), F32) + both((4, rows), BF) + both((rows,), BF, CUTS)
                + both((rows,), BF, tails) + both((rows,), BF) + both((rows,), BF)
                + both((rows,), BF, CUTS) + both((rows,), BF, tails))

    dacts, dw = pl.pallas_call(
        lambda *refs: kernel(n_norm, *refs),
        out_shape=(jax.ShapeDtypeStruct((2, 64, 384), BF),
                   jax.ShapeDtypeStruct((12, 27, 192), F32)),
        in_specs=[vm] * 5,
        out_specs=(vm, vm),
        scratch_shapes=[
            VMEM((2, 2, 64, 384), BF), VMEM((6, 6, 96, 128), BF),
            VMEM((2, 8, 128), F32), VMEM((2, 15, 8, 128), F32),
            VMEM((TAPK, 768), BF), VMEM((TAPK, 768), BF),
            VMEM((2, 192, 256), BF), VMEM((2, 192, 256), BF),
            VMEM((16, 3 * TAPK), F32), VMEM((2, 16, 3 * TAPK), F32),
            *both((4, 16), BF), *both((4, 48), BF), *ring(48), *ring(16),
            VMEM((32, 8, 128), F32), VMEM((3, 8, 8, 128), F32), VMEM((8, 8, 128), F32),
            VMEM((2, 32, 8, 128), F32),
            VMEM((2, 192, 256), F32), VMEM((192, 256), F32), VMEM((192, 512), F32),
            VMEM((2, 2, 64, 384), BF), VMEM((2, 64, 384), BF),
            dma, dma,
        ],
        compiler_params=pltpu.CompilerParams(
            collective_id=0, has_side_effects=True, vmem_limit_bytes=60 * 1024 * 1024),
        name="backward",
    )(acts2, cot, weights, gamma, beta)
    return dacts.reshape(2, 1, 64, 384), dw


def solution(mesh):
    placed = (
        P("block", "tile", None, None),
        P(),
        P(),
        P("tile", None, None),
        P("block", "tile", None, None),
    )
    return jax.shard_map(
        shards,
        mesh=mesh,
        in_specs=placed,
        out_specs=(P("block", "tile", None, None), P("tile", None, None)),
        check_vma=False,
    )
```

```python
import jax
import jax.numpy as jnp
from jax import lax
from jax.experimental import pallas as pl
from jax.experimental.pallas import tpu as pltpu
from jax.sharding import PartitionSpec as P

GROUPS = 32
NORM_EPS = 1e-06
MESH = pl.DeviceIdType.MESH
BF = jnp.bfloat16
F32 = jnp.float32
VMEM = pltpu.VMEM
NCOPY = 110
TAPK = 896
LANES = (1408, 1280)
CUTS = (768, 640)
SEGMENTS = (((0, 0, 896, 0), (1, 0, 512, 896)), ((1, 512, 384, 0), (2, 0, 896, 384)))


def iota(shape, dim):
    return lax.broadcasted_iota(jnp.int32, shape, dim)


def div12(v):
    return (v * 5462) >> 16


def kernel(n_norm, acts, cot_hbm, w_hbm, gamma_hbm, beta_hbm, dacts, dw,
           cot, w, gamma, beta, load_sem, actbuf, cotbuf, stat_out, stat_in, ghi, glo, hbuf, hswap, wflat,
           wy0, wy1, wx0, wx1, dp0, dp1, sb0, sb1,
           r10, r11, r20, r21, ra0, ra1, rb0, rb1, sm0, sm1, sn0, sn1,
           ep0, ep1, eb0, eb1, q10, q11, q20, q21, ea0, ea1, ec0, ec1, tm0, tm1, tn0, tn1,
           fin, zin, zred, zout, actp, actin, perm_scr, dsend, drecv, send_sem, recv_sem):
    z = lax.axis_index("block")
    tile = lax.axis_index("tile")
    core = lax.rem(tile, 2)
    q = lax.div(tile, 2)
    y = lax.rem(q, 4)
    x = lax.div(q, 4)
    u = lax.rem(z, 2)
    pair = lax.div(z, 2)
    wy, wx = (wy0, wy1), (wx0, wx1)

    def chip(cx, cy):
        return {"tile": (cx * 4 + cy) * 2 + core}

    partner = {"tile": tile + 1 - 2 * core}
    outer = {"tile": lax.rem(tile + 2 * core - 1 + 32, 32)}
    xp, xm = chip(lax.rem(x + 1, 4), y), chip(lax.rem(x + 3, 4), y)
    yp, ym = chip(x, lax.rem(y + 1, 4)), chip(x, lax.rem(y + 3, 4))
    plane = [{"tile": lax.rem(q + d, 16) * 2 + core} for d in range(1, 16)]
    column = [{"block": lax.rem(z + k, 8)} for k in range(1, 8)]
    twin = {"block": z + 1 - 2 * u}

    copies = []
    count = [0]

    def make(src, dst, device, slot=None):
        k = count[0]
        count[0] += 1
        return pltpu.make_async_remote_copy(
            src_ref=src, dst_ref=dst, send_sem=send_sem.at[k],
            recv_sem=recv_sem.at[k if slot is None else slot],
            device_id=device, device_id_type=MESH)

    def copy(src, dst, device):
        c = make(src, dst, device)
        copies.append(c)
        c.start()
        return c

    own = pl.ds(1 + 2 * core, 2)
    mine, theirs, later = pl.ds(2 * u, 2), pl.ds(2 - 2 * u, 2), pl.ds(4, 2)
    half = pl.ds(pl.multiple_of(96 * u, 32), 96)
    other_half = pl.ds(pl.multiple_of(96 - 96 * u, 32), 96)
    loads = [pltpu.make_async_copy(a, b, load_sem.at[k]) for k, (a, b) in enumerate((
        (acts, actbuf.at[:, core]), (cot_hbm, cot), (w_hbm, w),
        (cot_hbm.at[:, :, half], cotbuf.at[mine, own]), (gamma_hbm, gamma), (beta_hbm, beta)))]
    for c in loads:
        c.start()

    barrier = pltpu.get_barrier_semaphore()
    friends = plane + column + [partner, outer]
    for dev in friends:
        pl.semaphore_signal(barrier, inc=1, device_id=dev, device_id_type=MESH)
    pl.semaphore_wait(barrier, len(friends))

    line, there = 5 * core, 5 * (1 - core)
    loads[0].wait()
    c_act = copy(actbuf.at[:, core], actbuf.at[:, core], partner)
    loads[1].wait()
    edge_row, inner_row = 1 + 3 * core, 2 + core
    nexts, c_twin, c_next = [], [], []
    for r, dst_row in ((core, edge_row), (1 - core, inner_row)):
        slot = count[0]
        c_next.append(make(cot.at[:, r, pl.ds(0, 96)], cotbuf.at[later, dst_row], column[5], slot))
        nexts.append(c_next[-1])
        nexts.append(make(cot.at[:, r, pl.ds(96, 96)], cotbuf.at[later, dst_row], column[6], slot))

        @pl.when(u == 0)
        def _(pair_=nexts[-2:]):
            for c in pair_:
                c.start()

        c_twin.append(copy(cot.at[:, r, other_half], cotbuf.at[mine, dst_row], twin))

    c_pair = copy(cot.at[:, :, half], cotbuf.at[mine, own], partner)
    c_edge = copy(cot.at[:, core, half], cotbuf.at[mine, there], outer)

    places = ((y, yp, ym, x, xp, xm), (x, xp, xm, y, yp, ym))

    def gather_start(buf, p, plus, minus):
        return copy(buf.at[p], buf.at[p], plus), copy(buf.at[p], buf.at[p], minus)

    def gather_forward(h, buf, p, plus, minus, pair_):
        lo, hi = pl.ds(0, CUTS[h]), pl.ds(CUTS[h], LANES[h] - CUTS[h])
        pair_[0].wait_recv()
        low = lax.rem(p + 3, 4)
        f1 = copy(buf.at[low, :, lo], buf.at[low, :, lo], plus)
        pair_[1].wait_recv()
        high = lax.rem(p + 1, 4)
        f2 = copy(buf.at[high, :, hi], buf.at[high, :, hi], minus)
        return f1, f2

    first = []
    loads[2].wait()
    wide_w = w[...].astype(F32)
    wide_w = jnp.where(u == 0, wide_w[..., 0:96], wide_w[..., 96:192])
    for a in range(3):
        for b in range(9):
            k = a * TAPK + 96 * b
            wflat[0:12, k:k + 96] = wide_w[:, 9 * a + b, :]
        wflat[0:12, a * TAPK + 864:a * TAPK + TAPK] = jnp.zeros((12, 32), F32)
    for h in range(2):
        p, plus, minus = places[h][:3]
        wy[h][p] = wflat[:, 1408 * h:1408 * h + LANES[h]].astype(BF)
        first.append(gather_start(wy[h], p, plus, minus))

    for c in loads[3:]:
        c.wait()
    blk = div12(iota((192, 384), 0))
    pick = iota((192, 384), 1) == iota((192, 384), 0) + 12 * blk + 12 * core
    pick_bf = jnp.where(pick, 1.0, 0.0).astype(BF)
    gcol = jnp.sum(jnp.where(pick, gamma[...][None, :], 0.0), axis=1, keepdims=True)
    bcol = jnp.sum(jnp.where(pick, beta[...][None, :], 0.0), axis=1, keepdims=True)
    member = iota((192, 128), 1) == div12(iota((192, 128), 0))
    c_act.wait_recv()
    xt = lax.dot_general(pick_bf, actbuf[...].reshape(256, 384), (((1,), (1,)), ((), ())),
                         preferred_element_type=F32)

    def group_sums(a, b):
        lines = []
        for value in (a, b):
            for t in range(2):
                c = jnp.sum(value[:, 128 * t:128 * t + 128], axis=1, keepdims=True)
                lines.append(jnp.sum(jnp.where(member, c, 0.0), axis=0, keepdims=True))
        return jnp.concatenate(lines + [jnp.zeros((4, 128), F32)], axis=0)

    def spread(v):
        return jnp.sum(jnp.where(member, v, 0.0), axis=1, keepdims=True)

    def stats_start(k, total):
        stat_out[k] = total
        return [copy(stat_out.at[k], stat_in.at[k, d], plane[d]) for d in range(15)]

    def stats_end(k, total, cs):
        for d in range(15):
            cs[d].wait_recv()
            total = total + stat_in[k, d]
        return total

    tot1 = group_sums(xt, xt * xt)
    s1 = stats_start(0, tot1)

    def pass_edge(frames, c):
        c.wait_recv()
        return copy(cotbuf.at[frames, line], cotbuf.at[frames, line], partner)

    def pass_row(frames, r, device, to, c):
        if c is not None:
            c.wait_recv()
        return copy(cotbuf.at[frames, r], cotbuf.at[frames, to], device)

    early, late = [c_pair], []
    second = [gather_forward(h, wy[h], *places[h][:3], first[h]) for h in range(2)]
    early.append(pass_edge(mine, c_edge))
    edge1 = pass_row(theirs, edge_row, outer, there, c_twin[0])
    early.append(pass_row(theirs, edge_row, partner, edge_row, None))
    edge2 = pass_row(later, edge_row, outer, there, c_next[0])
    late.append(pass_row(later, edge_row, partner, edge_row, None))
    early.append(pass_row(theirs, inner_row, partner, inner_row, c_twin[1]))

    tot1 = stats_end(0, tot1, s1)
    mean_l = tot1[0:2] / n_norm
    inv_l = lax.rsqrt(tot1[2:4] / n_norm - mean_l * mean_l + NORM_EPS)
    wide = lambda m: jnp.concatenate(
        [jnp.broadcast_to(spread(m[t:t + 1]), (192, 128)) for t in range(2)], axis=1)
    inv = wide(inv_l)
    normed = (xt - wide(mean_l)) * inv
    shifted = normed * gcol + bcol
    gate = jax.nn.sigmoid(shifted)
    hidden = (shifted * gate).astype(BF)
    hbuf[u] = hidden
    c_hid = copy(hbuf.at[u], hbuf.at[u], twin)
    slope = gate * (1.0 + shifted * (1.0 - gate)) * gcol
    b2 = div12(iota((192, 192), 0))
    swap = iota((192, 192), 1) == iota((192, 192), 0) + 12 * ((b2 & 3) * 4 + (b2 >> 2) - b2)
    swap_bf = jnp.where(swap, 1.0, 0.0).astype(BF)
    hswap[u] = jnp.dot(swap_bf, hidden, preferred_element_type=F32).astype(BF)

    third = []
    for h in range(2):
        for f in second[h]:
            f.wait_recv()
        p2, plus2, minus2 = places[h][3:]
        parts = [wy[h][j].astype(F32)[0:12] for j in range(4)]
        wx[h][p2] = jnp.concatenate(parts, axis=0).astype(BF)
        third.append(gather_start(wx[h], p2, plus2, minus2))

    early.append(pass_edge(theirs, edge1))
    late.append(pass_row(later, inner_row, partner, inner_row, c_next[1]))
    late.append(pass_edge(later, edge2))
    for c in early:
        c.wait_recv()
    left = iota((96, 128), 1) < 64
    col, lane = iota((128, 384), 0), iota((128, 384), 1)
    shift = col - 2 * (lane & 63) + (lane >> 7) - 1
    summer = jnp.where((shift == 0) | (shift == 1), 1.0, 0.0).astype(BF)
    ghi[864:896] = jnp.zeros((32, 768), BF)
    glo[864:896] = jnp.zeros((32, 768), BF)
    for f in range(6):
        if f == 4:
            for c in late:
                c.wait_recv()
        sums = jnp.dot(cotbuf[f].reshape(576, 128), summer, preferred_element_type=F32)
        if f >= 4:
            sums = jnp.where(pair < 3, sums, 0.0)
        lines = [sums[96 * h:96 * h + 96] for h in range(6)]
        lines[0] = jnp.where(q > 0, lines[0], 0.0)
        lines[5] = jnp.where(q < 15, lines[5], 0.0)
        for e in range(3):
            ls = [v[:, 128 * e:128 * e + 128] for v in lines]
            for b in range(3):
                v = jnp.where(left, ls[2 - b] + ls[3 - b], ls[4 - b] + ls[5 - b])
                hi = v.astype(BF)
                k = (3 * b + e) * 96
                ghi[k:k + 96, 128 * f:128 * f + 128] = hi
                glo[k:k + 96, 128 * f:128 * f + 128] = (v - hi.astype(F32)).astype(BF)

    def reduce_start(h, part, sbuf, p, plus, minus, r1, r2, a_in, b_in):
        opp, nxt, prv = lax.rem(p + 2, 4), lax.rem(p + 1, 4), lax.rem(p + 3, 4)
        lo, hi = pl.ds(0, CUTS[h]), pl.ds(CUTS[h], LANES[h] - CUTS[h])
        sbuf[opp] = part[opp].astype(BF)
        o1 = copy(sbuf.at[opp, :, lo], r1, plus)
        o2 = copy(sbuf.at[opp, :, hi], r2, minus)
        sbuf[nxt] = part[nxt].astype(BF)
        n1 = copy(sbuf.at[nxt, :, hi], a_in.at[:, hi], plus)
        sbuf[prv] = part[prv].astype(BF)
        n2 = copy(sbuf.at[prv, :, lo], b_in.at[:, lo], minus)
        return o1, o2, n1, n2

    def reduce_mid(h, part, p, plus, minus, r1, r2, a_in, b_in, s_1, s_2, cs):
        nxt, prv = lax.rem(p + 1, 4), lax.rem(p + 3, 4)
        lo, hi = pl.ds(0, CUTS[h]), pl.ds(CUTS[h], LANES[h] - CUTS[h])
        cs[0].wait_recv()
        s_1[...] = (part[nxt, :, lo] + r1[...].astype(F32)).astype(BF)
        m1 = copy(s_1, a_in.at[:, lo], plus)
        cs[1].wait_recv()
        s_2[...] = (part[prv, :, hi] + r2[...].astype(F32)).astype(BF)
        m2 = copy(s_2, b_in.at[:, hi], minus)
        return m1, m2

    def reduce_end(part, p, a_in, b_in, cs, ms):
        for c in (cs[2], cs[3], ms[0], ms[1]):
            c.wait_recv()
        return part[p] + a_in[...].astype(F32) + b_in[...].astype(F32)

    rs_places = (places[1], places[0])
    hid = (hbuf, hswap)
    dp, sb = (dp0, dp1), (sb0, sb1)
    rs_in = ((r10, r20, ra0, rb0), (r11, r21, ra1, rb1))
    rs_mid = ((sm0, sn0), (sm1, sn1))

    def partial(h, v):
        outs = []
        for a, k0, rows, _ in SEGMENTS[h]:
            lanes = pl.ds(pl.multiple_of(256 * v + (2 - a) * 128, 128), 256)
            acc = None
            for g in (ghi, glo):
                d = lax.dot_general(hid[h][v], g[k0:k0 + rows, lanes], (((1,), (1,)), ((), ())),
                                    preferred_element_type=F32)
                acc = d if acc is None else acc + d
            outs.append(acc)
        return outs

    for h in range(2):
        for (a, k0, rows, l0), d in zip(SEGMENTS[h], partial(h, u)):
            for j in range(4):
                dp[h][j, :, l0:l0 + rows] = d[48 * j:48 * j + 48]
    c_hid.wait_recv()
    hswap[1 - u] = jnp.dot(swap_bf, hbuf[1 - u], preferred_element_type=F32).astype(BF)
    started = []
    for h in range(2):
        for (a, k0, rows, l0), d in zip(SEGMENTS[h], partial(h, 1 - u)):
            for j in range(4):
                dp[h][j, :, l0:l0 + rows] += d[48 * j:48 * j + 48]
        p, plus, minus = rs_places[h][:3]
        started.append(reduce_start(h, dp[h], sb[h], p, plus, minus, *rs_in[h]))

    fourth = [gather_forward(h, wx[h], *places[h][3:], third[h]) for h in range(2)]

    mids = []
    for h in range(2):
        p, plus, minus = rs_places[h][:3]
        mids.append(reduce_mid(h, dp[h], p, plus, minus, *rs_in[h], *rs_mid[h], started[h]))

    ag = []
    for h in range(2):
        for f in fourth[h]:
            f.wait_recv()
        acc = jnp.zeros((192, 512), F32)
        for a, k0, rows, l0 in SEGMENTS[h]:
            wa = jnp.concatenate([wx[h][j, :, l0:l0 + rows] for j in range(4)], axis=0)
            for g in (ghi, glo):
                acc = acc + jnp.dot(wa, g[k0:k0 + rows, (2 - a) * 128:(2 - a) * 128 + 512],
                                    preferred_element_type=F32)
        ag.append(acc)
    for m in range(16):
        b = (m % 4) * 4 + m // 4
        perm_scr[12 * m:12 * m + 12, :] = ag[1][12 * b:12 * b + 12]
    for v in range(2):
        actp[v] = ag[0][:, 256 * v:256 * v + 256] + perm_scr[:, 256 * v:256 * v + 256]
    c_grad = copy(actp.at[1 - u], actin, twin)

    ep, eb = (ep0, ep1), (eb0, eb1)
    rs_in2 = ((q10, q20, ea0, ec0), (q11, q21, ea1, ec1))
    rs_mid2 = ((tm0, tn0), (tm1, tn1))
    second_rs = []
    for h in range(2):
        p = rs_places[h][0]
        whole = reduce_end(dp[h], p, rs_in[h][2], rs_in[h][3], started[h], mids[h])
        for j in range(4):
            ep[h][j, 8:16] = jnp.zeros((8, LANES[h]), F32)
            ep[h][j, 0:12] = whole[12 * j:12 * j + 12]
        p2, plus2, minus2 = rs_places[h][3:]
        second_rs.append(reduce_start(h, ep[h], eb[h], p2, plus2, minus2, *rs_in2[h]))
    mids2 = []
    for h in range(2):
        p2, plus2, minus2 = rs_places[h][3:]
        mids2.append(reduce_mid(h, ep[h], p2, plus2, minus2, *rs_in2[h], *rs_mid2[h],
                                second_rs[h]))

    rest = []
    for h in range(2):
        p2 = rs_places[h][3]
        done = reduce_end(ep[h], p2, rs_in2[h][2], rs_in2[h][3], second_rs[h], mids2[h])
        for k in range(LANES[h] // 128):
            fin[11 * h + k] = done[0:8, 128 * k:128 * k + 128]
            rest.append(done[8:12, 128 * k:128 * k + 128])
    rest.append(jnp.zeros((4, 128), F32))
    for m in range(11):
        fin[21 + m] = jnp.concatenate([rest[2 * m], rest[2 * m + 1]], axis=0)

    zs = []
    for m in range(1, 4):
        owner = lax.rem(pair + m, 4)
        zs.append(copy(fin.at[pl.ds(8 * owner, 8)], zin.at[m - 1], column[2 * m - 1]))
    c_grad.wait_recv()
    norm_grad = (actp[u] + actin[...]) * slope
    tot2 = group_sums(norm_grad, norm_grad * normed)
    s2 = stats_start(1, tot2)

    total = fin[pl.ds(8 * pair, 8)]
    for m in range(3):
        zs[m].wait_recv()
        total = total + zin[m]
    zred[...] = total
    zg = [copy(zred, zout.at[u, pl.ds(8 * pair, 8)], column[k]) for k in range(7)]
    zout[u, pl.ds(8 * pair, 8)] = total
    tot2 = stats_end(1, tot2, s2)
    mean2 = tot2[0:4] / n_norm
    d = inv * (norm_grad - wide(mean2[0:2]) - normed * wide(mean2[2:4]))
    back = lax.dot_general(d.astype(BF), pick_bf, (((0,), (0,)), ((), ())),
                           preferred_element_type=F32)
    dsend[...] = back.astype(BF).reshape(2, 2, 64, 384)
    c_out = copy(dsend.at[:, 1 - core], drecv, partner)

    c_out.wait_recv()
    dacts[...] = dsend[:, core] + drecv[...]
    for c in zg:
        c.wait_recv()
    dw[...] = zout[...]
    for c in copies:
        c.wait_send()

    @pl.when(u == 0)
    def _():
        for c in nexts:
            c.wait_send()


def finish(dacts_in, zout, dacts, dw, dflat):
    dacts[...] = dacts_in[...]
    for v in range(2):
        for k in range(21):
            dflat[v, 0:8, 128 * k:128 * k + 128] = zout[v, k]
        for m in range(11):
            two = zout[v, 21 + m]
            dflat[v, 8:12, 256 * m:256 * m + 128] = two[0:4]
            if m < 10:
                dflat[v, 8:12, 256 * m + 128:256 * m + 256] = two[4:8]
    for a in range(3):
        for b in range(9):
            k = a * TAPK + 96 * b
            dw[:, 9 * a + b, 0:96] = dflat[0, 0:12, k:k + 96]
            dw[:, 9 * a + b, 96:192] = dflat[1, 0:12, k:k + 96]


def shards(acts, gamma, beta, weights, cotangent):
    frames, low_rows, low_cols, channels = acts.shape
    n_norm = float(low_rows * 32 * low_cols * (channels // GROUPS))
    acts2 = acts.reshape(2, 64, 384)
    cot = cotangent.swapaxes(2, 3)
    vm = pl.BlockSpec(memory_space=VMEM)
    dma = pltpu.SemaphoreType.DMA((NCOPY,))
    both = lambda lead, dtype, lanes=LANES: [VMEM((*lead, n), dtype) for n in lanes]
    tails = tuple(n - c for n, c in zip(LANES, CUTS))

    def ring(rows):
        return (both((4, rows), F32) + both((4, rows), BF) + both((rows,), BF, CUTS)
                + both((rows,), BF, tails) + both((rows,), BF) + both((rows,), BF)
                + both((rows,), BF, CUTS) + both((rows,), BF, tails))

    dacts, dw = pl.pallas_call(
        lambda *refs: kernel(n_norm, *refs),
        out_shape=(jax.ShapeDtypeStruct((2, 64, 384), BF),
                   jax.ShapeDtypeStruct((2, 32, 8, 128), F32)),
        in_specs=[pl.BlockSpec(memory_space=pl.ANY)] * 5,
        out_specs=(vm, vm),
        scratch_shapes=[
            VMEM((2, 2, 192, 128), BF), VMEM((12, 27, 192), BF), VMEM((384,), F32),
            VMEM((384,), F32), pltpu.SemaphoreType.DMA((6,)),
            VMEM((2, 2, 64, 384), BF), VMEM((6, 6, 96, 128), BF),
            VMEM((2, 8, 128), F32), VMEM((2, 15, 8, 128), F32),
            VMEM((TAPK, 768), BF), VMEM((TAPK, 768), BF),
            VMEM((2, 192, 256), BF), VMEM((2, 192, 256), BF),
            VMEM((16, 3 * TAPK), F32),
            *both((4, 16), BF), *both((4, 48), BF), *ring(48), *ring(16),
            VMEM((32, 8, 128), F32), VMEM((3, 8, 8, 128), F32), VMEM((8, 8, 128), F32),
            VMEM((2, 32, 8, 128), F32),
            VMEM((2, 192, 256), F32), VMEM((192, 256), F32), VMEM((192, 512), F32),
            VMEM((2, 2, 64, 384), BF), VMEM((2, 64, 384), BF),
            dma, dma,
        ],
        compiler_params=pltpu.CompilerParams(
            collective_id=0, has_side_effects=True, vmem_limit_bytes=20 * 1024 * 1024),
        name="backward",
    )(acts2, cot, weights, gamma, beta)
    dacts, dw = pl.pallas_call(
        finish,
        out_shape=(jax.ShapeDtypeStruct((2, 64, 384), BF),
                   jax.ShapeDtypeStruct((12, 27, 192), F32)),
        in_specs=[vm] * 2,
        out_specs=(vm, vm),
        scratch_shapes=[VMEM((2, 16, 3 * TAPK), F32)],
        compiler_params=pltpu.CompilerParams(vmem_limit_bytes=8 * 1024 * 1024),
        name="finish",
    )(dacts, dw)
    return dacts.reshape(2, 1, 64, 384), dw


def solution(mesh):
    placed = (
        P("block", "tile", None, None),
        P(),
        P(),
        P("tile", None, None),
        P("block", "tile", None, None),
    )
    return jax.shard_map(
        shards,
        mesh=mesh,
        in_specs=placed,
        out_specs=(P("block", "tile", None, None), P("tile", None, None)),
        check_vma=False,
    )
```

```python
import jax
import jax.numpy as jnp
from jax import lax
from jax.experimental import pallas as pl
from jax.experimental.pallas import tpu as pltpu
from jax.sharding import PartitionSpec as P

GROUPS = 32
NORM_EPS = 1e-06
MESH = pl.DeviceIdType.MESH
BF = jnp.bfloat16
F32 = jnp.float32
VMEM = pltpu.VMEM
NCOPY = 110
TAPK = 896
LANES = (1408, 1280)
CUTS = (768, 640)
SEGMENTS = (((0, 0, 896, 0), (1, 0, 512, 896)), ((1, 512, 384, 0), (2, 0, 896, 384)))


def iota(shape, dim):
    return lax.broadcasted_iota(jnp.int32, shape, dim)


def div12(v):
    return (v * 5462) >> 16


def kernel(n_norm, acts, cot_hbm, w_hbm, gamma_hbm, beta_hbm, dacts, dw,
           cot, w, gamma, beta, load_sem, actbuf, cotbuf, stat_out, stat_in, ghi, glo, hbuf, hswap, wflat,
           wy0, wy1, wx0, wx1, dp0, dp1, sb0, sb1,
           r10, r11, r20, r21, ra0, ra1, rb0, rb1, sm0, sm1, sn0, sn1,
           ep0, ep1, q10, q11, q20, q21, ea0, ea1, ec0, ec1, tm0, tm1, tn0, tn1,
           fin, zin, zred, zout, actp, actin, perm_scr, dsend, drecv, send_sem, recv_sem):
    z = lax.axis_index("block")
    tile = lax.axis_index("tile")
    core = lax.rem(tile, 2)
    q = lax.div(tile, 2)
    y = lax.rem(q, 4)
    x = lax.div(q, 4)
    u = lax.rem(z, 2)
    pair = lax.div(z, 2)
    wy, wx = (wy0, wy1), (wx0, wx1)

    def chip(cx, cy):
        return {"tile": (cx * 4 + cy) * 2 + core}

    partner = {"tile": tile + 1 - 2 * core}
    outer = {"tile": lax.rem(tile + 2 * core - 1 + 32, 32)}
    xp, xm = chip(lax.rem(x + 1, 4), y), chip(lax.rem(x + 3, 4), y)
    yp, ym = chip(x, lax.rem(y + 1, 4)), chip(x, lax.rem(y + 3, 4))
    plane = [{"tile": lax.rem(q + d, 16) * 2 + core} for d in range(1, 16)]
    column = [{"block": lax.rem(z + k, 8)} for k in range(1, 8)]
    twin = {"block": z + 1 - 2 * u}

    copies = []
    count = [0]

    def make(src, dst, device, slot=None):
        k = count[0]
        count[0] += 1
        return pltpu.make_async_remote_copy(
            src_ref=src, dst_ref=dst, send_sem=send_sem.at[k],
            recv_sem=recv_sem.at[k if slot is None else slot],
            device_id=device, device_id_type=MESH)

    def copy(src, dst, device):
        c = make(src, dst, device)
        copies.append(c)
        c.start()
        return c

    own = pl.ds(1 + 2 * core, 2)
    mine, theirs, later = pl.ds(2 * u, 2), pl.ds(2 - 2 * u, 2), pl.ds(4, 2)
    half = pl.ds(pl.multiple_of(96 * u, 32), 96)
    other_half = pl.ds(pl.multiple_of(96 - 96 * u, 32), 96)
    loads = [pltpu.make_async_copy(a, b, load_sem.at[k]) for k, (a, b) in enumerate((
        (acts, actbuf.at[:, core]), (cot_hbm, cot), (w_hbm, w),
        (cot_hbm.at[:, :, half], cotbuf.at[mine, own]), (gamma_hbm, gamma), (beta_hbm, beta)))]
    for c in loads:
        c.start()

    barrier = pltpu.get_barrier_semaphore()
    friends = plane + column + [partner, outer]
    for dev in friends:
        pl.semaphore_signal(barrier, inc=1, device_id=dev, device_id_type=MESH)
    pl.semaphore_wait(barrier, len(friends))

    line, there = 5 * core, 5 * (1 - core)
    loads[0].wait()
    c_act = copy(actbuf.at[:, core], actbuf.at[:, core], partner)
    loads[1].wait()
    edge_row, inner_row = 1 + 3 * core, 2 + core
    nexts, c_twin, c_next = [], [], []
    for r, dst_row in ((core, edge_row), (1 - core, inner_row)):
        slot = count[0]
        c_next.append(make(cot.at[:, r, pl.ds(0, 96)], cotbuf.at[later, dst_row], column[5], slot))
        nexts.append(c_next[-1])
        nexts.append(make(cot.at[:, r, pl.ds(96, 96)], cotbuf.at[later, dst_row], column[6], slot))

        @pl.when(u == 0)
        def _(pair_=nexts[-2:]):
            for c in pair_:
                c.start()

        c_twin.append(copy(cot.at[:, r, other_half], cotbuf.at[mine, dst_row], twin))

    c_pair = copy(cot.at[:, :, half], cotbuf.at[mine, own], partner)
    c_edge = copy(cot.at[:, core, half], cotbuf.at[mine, there], outer)

    places = ((y, yp, ym, x, xp, xm), (x, xp, xm, y, yp, ym))

    def gather_start(buf, p, plus, minus):
        return copy(buf.at[p], buf.at[p], plus), copy(buf.at[p], buf.at[p], minus)

    def gather_forward(h, buf, p, plus, minus, pair_):
        lo, hi = pl.ds(0, CUTS[h]), pl.ds(CUTS[h], LANES[h] - CUTS[h])
        pair_[0].wait_recv()
        low = lax.rem(p + 3, 4)
        f1 = copy(buf.at[low, :, lo], buf.at[low, :, lo], plus)
        pair_[1].wait_recv()
        high = lax.rem(p + 1, 4)
        f2 = copy(buf.at[high, :, hi], buf.at[high, :, hi], minus)
        return f1, f2

    first = []
    loads[2].wait()
    wide_w = w[...].astype(F32)
    wide_w = jnp.where(u == 0, wide_w[..., 0:96], wide_w[..., 96:192])
    for a in range(3):
        for b in range(9):
            k = a * TAPK + 96 * b
            wflat[0:12, k:k + 96] = wide_w[:, 9 * a + b, :]
        wflat[0:12, a * TAPK + 864:a * TAPK + TAPK] = jnp.zeros((12, 32), F32)
    for h in range(2):
        p, plus, minus = places[h][:3]
        wy[h][p] = wflat[:, 1408 * h:1408 * h + LANES[h]].astype(BF)
        first.append(gather_start(wy[h], p, plus, minus))

    for c in loads[3:]:
        c.wait()
    blk = div12(iota((192, 384), 0))
    pick = iota((192, 384), 1) == iota((192, 384), 0) + 12 * blk + 12 * core
    pick_bf = jnp.where(pick, 1.0, 0.0).astype(BF)
    gcol = jnp.sum(jnp.where(pick, gamma[...][None, :], 0.0), axis=1, keepdims=True)
    bcol = jnp.sum(jnp.where(pick, beta[...][None, :], 0.0), axis=1, keepdims=True)
    member = iota((192, 128), 1) == div12(iota((192, 128), 0))
    c_act.wait_recv()
    xt = lax.dot_general(pick_bf, actbuf[...].reshape(256, 384), (((1,), (1,)), ((), ())),
                         preferred_element_type=F32)

    def group_sums(a, b):
        lines = []
        for value in (a, b):
            for t in range(2):
                c = jnp.sum(value[:, 128 * t:128 * t + 128], axis=1, keepdims=True)
                lines.append(jnp.sum(jnp.where(member, c, 0.0), axis=0, keepdims=True))
        return jnp.concatenate(lines + [jnp.zeros((4, 128), F32)], axis=0)

    def spread(v):
        return jnp.sum(jnp.where(member, v, 0.0), axis=1, keepdims=True)

    def stats_start(k, total):
        stat_out[k] = total
        return [copy(stat_out.at[k], stat_in.at[k, d], plane[d]) for d in range(15)]

    def stats_end(k, total, cs):
        for d in range(15):
            cs[d].wait_recv()
            total = total + stat_in[k, d]
        return total

    tot1 = group_sums(xt, xt * xt)
    s1 = stats_start(0, tot1)

    def pass_edge(frames, c):
        c.wait_recv()
        return copy(cotbuf.at[frames, line], cotbuf.at[frames, line], partner)

    def pass_row(frames, r, device, to, c):
        if c is not None:
            c.wait_recv()
        return copy(cotbuf.at[frames, r], cotbuf.at[frames, to], device)

    early, late = [c_pair], []
    second = [gather_forward(h, wy[h], *places[h][:3], first[h]) for h in range(2)]
    early.append(pass_edge(mine, c_edge))
    edge1 = pass_row(theirs, edge_row, outer, there, c_twin[0])
    early.append(pass_row(theirs, edge_row, partner, edge_row, None))
    edge2 = pass_row(later, edge_row, outer, there, c_next[0])
    late.append(pass_row(later, edge_row, partner, edge_row, None))
    early.append(pass_row(theirs, inner_row, partner, inner_row, c_twin[1]))

    tot1 = stats_end(0, tot1, s1)
    mean_l = tot1[0:2] / n_norm
    inv_l = lax.rsqrt(tot1[2:4] / n_norm - mean_l * mean_l + NORM_EPS)
    wide = lambda m: jnp.concatenate(
        [jnp.broadcast_to(spread(m[t:t + 1]), (192, 128)) for t in range(2)], axis=1)
    inv = wide(inv_l)
    normed = (xt - wide(mean_l)) * inv
    shifted = normed * gcol + bcol
    gate = jax.nn.sigmoid(shifted)
    hidden = (shifted * gate).astype(BF)
    hbuf[u] = hidden
    c_hid = copy(hbuf.at[u], hbuf.at[u], twin)
    slope = gate * (1.0 + shifted * (1.0 - gate)) * gcol
    b2 = div12(iota((192, 192), 0))
    swap = iota((192, 192), 1) == iota((192, 192), 0) + 12 * ((b2 & 3) * 4 + (b2 >> 2) - b2)
    swap_bf = jnp.where(swap, 1.0, 0.0).astype(BF)
    hswap[u] = jnp.dot(swap_bf, hidden, preferred_element_type=F32).astype(BF)

    early.append(pass_edge(theirs, edge1))
    late.append(pass_row(later, inner_row, partner, inner_row, c_next[1]))
    late.append(pass_edge(later, edge2))
    third = []
    for h in range(2):
        for f in second[h]:
            f.wait_recv()
        p2, plus2, minus2 = places[h][3:]
        parts = [wy[h][j].astype(F32)[0:12] for j in range(4)]
        wx[h][p2] = jnp.concatenate(parts, axis=0).astype(BF)
        third.append(gather_start(wx[h], p2, plus2, minus2))

    for c in early:
        c.wait_recv()
    left = iota((96, 128), 1) < 64
    col, lane = iota((128, 384), 0), iota((128, 384), 1)
    shift = col - 2 * (lane & 63) + (lane >> 7) - 1
    summer = jnp.where((shift == 0) | (shift == 1), 1.0, 0.0).astype(BF)
    ghi[864:896] = jnp.zeros((32, 768), BF)
    glo[864:896] = jnp.zeros((32, 768), BF)
    for f in range(6):
        if f == 4:
            for c in late:
                c.wait_recv()
        sums = jnp.dot(cotbuf[f].reshape(576, 128), summer, preferred_element_type=F32)
        if f >= 4:
            sums = jnp.where(pair < 3, sums, 0.0)
        lines = [sums[96 * h:96 * h + 96] for h in range(6)]
        lines[0] = jnp.where(q > 0, lines[0], 0.0)
        lines[5] = jnp.where(q < 15, lines[5], 0.0)
        for e in range(3):
            ls = [v[:, 128 * e:128 * e + 128] for v in lines]
            for b in range(3):
                v = jnp.where(left, ls[2 - b] + ls[3 - b], ls[4 - b] + ls[5 - b])
                hi = v.astype(BF)
                k = (3 * b + e) * 96
                ghi[k:k + 96, 128 * f:128 * f + 128] = hi
                glo[k:k + 96, 128 * f:128 * f + 128] = (v - hi.astype(F32)).astype(BF)

    def reduce_start(h, part, sbuf, p, plus, minus, r1, r2, a_in, b_in):
        opp, nxt, prv = lax.rem(p + 2, 4), lax.rem(p + 1, 4), lax.rem(p + 3, 4)
        lo, hi = pl.ds(0, CUTS[h]), pl.ds(CUTS[h], LANES[h] - CUTS[h])
        if sbuf is not part:
            sbuf[opp] = part[opp].astype(BF)
        o1 = copy(sbuf.at[opp, :, lo], r1, plus)
        o2 = copy(sbuf.at[opp, :, hi], r2, minus)
        if sbuf is not part:
            sbuf[nxt] = part[nxt].astype(BF)
        n1 = copy(sbuf.at[nxt, :, hi], a_in.at[:, hi], plus)
        if sbuf is not part:
            sbuf[prv] = part[prv].astype(BF)
        n2 = copy(sbuf.at[prv, :, lo], b_in.at[:, lo], minus)
        return o1, o2, n1, n2

    def reduce_mid(h, part, p, plus, minus, r1, r2, a_in, b_in, s_1, s_2, cs):
        nxt, prv = lax.rem(p + 1, 4), lax.rem(p + 3, 4)
        lo, hi = pl.ds(0, CUTS[h]), pl.ds(CUTS[h], LANES[h] - CUTS[h])
        cs[0].wait_recv()
        s_1[...] = (part[nxt, :, lo] + r1[...].astype(F32)).astype(s_1.dtype)
        m1 = copy(s_1, a_in.at[:, lo], plus)
        cs[1].wait_recv()
        s_2[...] = (part[prv, :, hi] + r2[...].astype(F32)).astype(s_2.dtype)
        m2 = copy(s_2, b_in.at[:, hi], minus)
        return m1, m2

    def reduce_end(part, p, a_in, b_in, cs, ms):
        for c in (cs[2], cs[3], ms[0], ms[1]):
            c.wait_recv()
        return part[p] + a_in[...].astype(F32) + b_in[...].astype(F32)

    rs_places = (places[1], places[0])
    hid = (hbuf, hswap)
    dp, sb = (dp0, dp1), (sb0, sb1)
    rs_in = ((r10, r20, ra0, rb0), (r11, r21, ra1, rb1))
    rs_mid = ((sm0, sn0), (sm1, sn1))

    def partial(h, v):
        outs = []
        for a, k0, rows, _ in SEGMENTS[h]:
            lanes = pl.ds(pl.multiple_of(256 * v + (2 - a) * 128, 128), 256)
            acc = None
            for g in (ghi, glo):
                d = lax.dot_general(hid[h][v], g[k0:k0 + rows, lanes], (((1,), (1,)), ((), ())),
                                    preferred_element_type=F32)
                acc = d if acc is None else acc + d
            outs.append(acc)
        return outs

    for h in range(2):
        for (a, k0, rows, l0), d in zip(SEGMENTS[h], partial(h, u)):
            for j in range(4):
                dp[h][j, :, l0:l0 + rows] = d[48 * j:48 * j + 48]
    c_hid.wait_recv()
    hswap[1 - u] = jnp.dot(swap_bf, hbuf[1 - u], preferred_element_type=F32).astype(BF)
    started = []
    for h in range(2):
        for (a, k0, rows, l0), d in zip(SEGMENTS[h], partial(h, 1 - u)):
            for j in range(4):
                dp[h][j, :, l0:l0 + rows] += d[48 * j:48 * j + 48]
        p, plus, minus = rs_places[h][:3]
        started.append(reduce_start(h, dp[h], sb[h], p, plus, minus, *rs_in[h]))

    fourth = [gather_forward(h, wx[h], *places[h][3:], third[h]) for h in range(2)]

    mids = []
    for h in range(2):
        p, plus, minus = rs_places[h][:3]
        mids.append(reduce_mid(h, dp[h], p, plus, minus, *rs_in[h], *rs_mid[h], started[h]))

    ep = (ep0, ep1)
    rs_in2 = ((q10, q20, ea0, ec0), (q11, q21, ea1, ec1))
    rs_mid2 = ((tm0, tn0), (tm1, tn1))
    second_rs = []
    for h in range(2):
        p = rs_places[h][0]
        whole = reduce_end(dp[h], p, rs_in[h][2], rs_in[h][3], started[h], mids[h])
        for j in range(4):
            ep[h][j] = whole[12 * j:12 * j + 12]
        p2, plus2, minus2 = rs_places[h][3:]
        second_rs.append(reduce_start(h, ep[h], ep[h], p2, plus2, minus2, *rs_in2[h]))
    ag = []
    for h in range(2):
        for f in fourth[h]:
            f.wait_recv()
        acc = jnp.zeros((192, 512), F32)
        for a, k0, rows, l0 in SEGMENTS[h]:
            wa = jnp.concatenate([wx[h][j, :, l0:l0 + rows] for j in range(4)], axis=0)
            for g in (ghi, glo):
                acc = acc + jnp.dot(wa, g[k0:k0 + rows, (2 - a) * 128:(2 - a) * 128 + 512],
                                    preferred_element_type=F32)
        ag.append(acc)
    for m in range(16):
        b = (m % 4) * 4 + m // 4
        perm_scr[12 * m:12 * m + 12, :] = ag[1][12 * b:12 * b + 12]
    for v in range(2):
        actp[v] = ag[0][:, 256 * v:256 * v + 256] + perm_scr[:, 256 * v:256 * v + 256]
    c_grad = copy(actp.at[1 - u], actin, twin)

    mids2 = []
    for h in range(2):
        p2, plus2, minus2 = rs_places[h][3:]
        mids2.append(reduce_mid(h, ep[h], p2, plus2, minus2, *rs_in2[h], *rs_mid2[h],
                                second_rs[h]))

    rest = []
    for h in range(2):
        p2 = rs_places[h][3]
        done = reduce_end(ep[h], p2, rs_in2[h][2], rs_in2[h][3], second_rs[h], mids2[h])
        for k in range(LANES[h] // 128):
            fin[11 * h + k] = done[0:8, 128 * k:128 * k + 128]
            rest.append(done[8:12, 128 * k:128 * k + 128])
    rest.append(jnp.zeros((4, 128), F32))
    for m in range(11):
        fin[21 + m] = jnp.concatenate([rest[2 * m], rest[2 * m + 1]], axis=0)

    zs = []
    for m in range(1, 4):
        owner = lax.rem(pair + m, 4)
        zs.append(copy(fin.at[pl.ds(8 * owner, 8)], zin.at[m - 1], column[2 * m - 1]))
    c_grad.wait_recv()
    norm_grad = (actp[u] + actin[...]) * slope
    tot2 = group_sums(norm_grad, norm_grad * normed)
    s2 = stats_start(1, tot2)

    total = fin[pl.ds(8 * pair, 8)]
    for m in range(3):
        zs[m].wait_recv()
        total = total + zin[m]
    total = total.reshape(4, 16, 128).astype(BF)
    zred[...] = total
    zg = [copy(zred, zout.at[u, pl.ds(4 * pair, 4)], column[k]) for k in range(7)]
    zout[u, pl.ds(4 * pair, 4)] = total
    tot2 = stats_end(1, tot2, s2)
    mean2 = tot2[0:4] / n_norm
    d = inv * (norm_grad - wide(mean2[0:2]) - normed * wide(mean2[2:4]))
    back = lax.dot_general(d.astype(BF), pick_bf, (((0,), (0,)), ((), ())),
                           preferred_element_type=F32)
    dsend[...] = back.astype(BF).reshape(2, 2, 64, 384)
    c_out = copy(dsend.at[:, 1 - core], drecv, partner)

    c_out.wait_recv()
    dacts[...] = dsend[:, core] + drecv[...]
    for c in zg:
        c.wait_recv()
    dw[...] = zout[...]
    for c in copies:
        c.wait_send()

    @pl.when(u == 0)
    def _():
        for c in nexts:
            c.wait_send()


def finish(dacts_in, zout, dacts, dw, dflat):
    dacts[...] = dacts_in[...]
    for v in range(2):
        tiles = zout[v].astype(F32).reshape(32, 8, 128)
        for k in range(21):
            dflat[v, 0:8, 128 * k:128 * k + 128] = tiles[k]
        for m in range(11):
            two = tiles[21 + m]
            dflat[v, 8:12, 256 * m:256 * m + 128] = two[0:4]
            if m < 10:
                dflat[v, 8:12, 256 * m + 128:256 * m + 256] = two[4:8]
    for a in range(3):
        for b in range(9):
            k = a * TAPK + 96 * b
            dw[:, 9 * a + b, 0:96] = dflat[0, 0:12, k:k + 96]
            dw[:, 9 * a + b, 96:192] = dflat[1, 0:12, k:k + 96]


def shards(acts, gamma, beta, weights, cotangent):
    frames, low_rows, low_cols, channels = acts.shape
    n_norm = float(low_rows * 32 * low_cols * (channels // GROUPS))
    acts2 = acts.reshape(2, 64, 384)
    cot = cotangent.swapaxes(2, 3)
    vm = pl.BlockSpec(memory_space=VMEM)
    dma = pltpu.SemaphoreType.DMA((NCOPY,))
    both = lambda lead, dtype, lanes=LANES: [VMEM((*lead, n), dtype) for n in lanes]
    tails = tuple(n - c for n, c in zip(LANES, CUTS))

    def ring(rows, dtype):
        first = both((4, rows), F32) + (both((4, rows), BF) if dtype == BF else [])
        return (first + both((rows,), dtype, CUTS) + both((rows,), dtype, tails)
                + both((rows,), dtype) + both((rows,), dtype)
                + both((rows,), dtype, CUTS) + both((rows,), dtype, tails))

    dacts, dw = pl.pallas_call(
        lambda *refs: kernel(n_norm, *refs),
        out_shape=(jax.ShapeDtypeStruct((2, 64, 384), BF),
                   jax.ShapeDtypeStruct((2, 16, 16, 128), BF)),
        in_specs=[pl.BlockSpec(memory_space=pltpu.HBM)] * 5,
        out_specs=(vm, vm),
        scratch_shapes=[
            VMEM((2, 2, 192, 128), BF), VMEM((12, 27, 192), BF), VMEM((384,), F32),
            VMEM((384,), F32), pltpu.SemaphoreType.DMA((6,)),
            VMEM((2, 2, 64, 384), BF), VMEM((6, 6, 96, 128), BF),
            VMEM((2, 8, 128), F32), VMEM((2, 15, 8, 128), F32),
            VMEM((TAPK, 768), BF), VMEM((TAPK, 768), BF),
            VMEM((2, 192, 256), BF), VMEM((2, 192, 256), BF),
            VMEM((16, 3 * TAPK), F32),
            *both((4, 16), BF), *both((4, 48), BF), *ring(48, BF), *ring(12, F32),
            VMEM((32, 8, 128), F32), VMEM((3, 8, 8, 128), F32), VMEM((4, 16, 128), BF),
            VMEM((2, 16, 16, 128), BF),
            VMEM((2, 192, 256), F32), VMEM((192, 256), F32), VMEM((192, 512), F32),
            VMEM((2, 2, 64, 384), BF), VMEM((2, 64, 384), BF),
            dma, dma,
        ],
        compiler_params=pltpu.CompilerParams(
            collective_id=0, has_side_effects=True, vmem_limit_bytes=20 * 1024 * 1024),
        name="backward",
    )(*(pltpu.with_memory_space_constraint(v, pltpu.HBM) for v in (acts2, cot, weights, gamma, beta)))
    dacts, dw = pl.pallas_call(
        finish,
        out_shape=(jax.ShapeDtypeStruct((2, 64, 384), BF),
                   jax.ShapeDtypeStruct((12, 27, 192), F32)),
        in_specs=[vm] * 2,
        out_specs=(vm, vm),
        scratch_shapes=[VMEM((2, 16, 3 * TAPK), F32)],
        compiler_params=pltpu.CompilerParams(vmem_limit_bytes=8 * 1024 * 1024),
        name="finish",
    )(dacts, dw)
    return dacts.reshape(2, 1, 64, 384), dw


def solution(mesh):
    placed = (
        P("block", "tile", None, None),
        P(),
        P(),
        P("tile", None, None),
        P("block", "tile", None, None),
    )
    return jax.shard_map(
        shards,
        mesh=mesh,
        in_specs=placed,
        out_specs=(P("block", "tile", None, None), P("tile", None, None)),
        check_vma=False,
    )
```

```python
import jax
import jax.numpy as jnp
from jax import lax
from jax.experimental import pallas as pl
from jax.experimental.pallas import tpu as pltpu
from jax.sharding import PartitionSpec as P

GROUPS = 32
NORM_EPS = 1e-06
MESH = pl.DeviceIdType.MESH
BF = jnp.bfloat16
F32 = jnp.float32
VMEM = pltpu.VMEM
NCOPY = 144
TAPK = 896
LANES = (1408, 1280)
CUTS = (768, 640)
SEGMENTS = (((0, 0, 896, 0), (1, 0, 512, 896)), ((1, 512, 384, 0), (2, 0, 896, 384)))
STREAMS = ((0, 0, 768, 384), (1, 0, 640, 384), (0, 768, 640, 384), (1, 640, 640, 384))
STREAM_SEGMENTS = (((0, 0, 768, 0),), ((1, 512, 384, 0), (2, 0, 256, 384)),
                   ((0, 768, 128, 0), (1, 0, 512, 128)), ((2, 256, 640, 0),))


def iota(shape, dim):
    return lax.broadcasted_iota(jnp.int32, shape, dim)


def div12(v):
    return (v * 5462) >> 16


def kernel(n_norm, acts, cot_hbm, w_hbm, gamma_hbm, beta_hbm, dacts, dw,
           cot, w, gamma, beta, load_sem, actbuf, cotbuf, stat_out, stat_in, ghi, glo, hbuf, hswap, wflat,
           wy0, wy1, wx0, wx1, *rest):
    dps, sbs, r1s, r2s, ras, rbs, m1s, m2s = (rest[4 * k:4 * k + 4] for k in range(8))
    eps, q1s, q2s, eas, ecs, t1s, t2s = (rest[32 + 4 * k:36 + 4 * k] for k in range(7))
    (fin_p, fin_q, zin_p, zin_q, zred_p, zred_q, zout_p, zout_q,
     actp, actin, perm_scr, dsend, drecv, send_sem, recv_sem) = rest[60:]
    z = lax.axis_index("block")
    tile = lax.axis_index("tile")
    core = lax.rem(tile, 2)
    q = lax.div(tile, 2)
    y = lax.rem(q, 4)
    x = lax.div(q, 4)
    u = lax.rem(z, 2)
    pair = lax.div(z, 2)
    wy, wx = (wy0, wy1), (wx0, wx1)

    def chip(cx, cy):
        return {"tile": (cx * 4 + cy) * 2 + core}

    partner = {"tile": tile + 1 - 2 * core}
    outer = {"tile": lax.rem(tile + 2 * core - 1 + 32, 32)}
    xp, xm = chip(lax.rem(x + 1, 4), y), chip(lax.rem(x + 3, 4), y)
    yp, ym = chip(x, lax.rem(y + 1, 4)), chip(x, lax.rem(y + 3, 4))
    plane = [{"tile": lax.rem(q + d, 16) * 2 + core} for d in range(1, 16)]
    column = [{"block": lax.rem(z + k, 8)} for k in range(1, 8)]
    twin = {"block": z + 1 - 2 * u}

    copies = []
    count = [0]

    def make(src, dst, device, slot=None):
        k = count[0]
        count[0] += 1
        return pltpu.make_async_remote_copy(
            src_ref=src, dst_ref=dst, send_sem=send_sem.at[k],
            recv_sem=recv_sem.at[k if slot is None else slot],
            device_id=device, device_id_type=MESH)

    def copy(src, dst, device):
        c = make(src, dst, device)
        copies.append(c)
        c.start()
        return c

    own = pl.ds(1 + 2 * core, 2)
    mine, theirs, later = pl.ds(2 * u, 2), pl.ds(2 - 2 * u, 2), pl.ds(4, 2)
    half = pl.ds(pl.multiple_of(96 * u, 32), 96)
    other_half = pl.ds(pl.multiple_of(96 - 96 * u, 32), 96)
    loads = [pltpu.make_async_copy(a, b, load_sem.at[k]) for k, (a, b) in enumerate((
        (acts, actbuf.at[:, core]), (cot_hbm, cot), (w_hbm, w),
        (cot_hbm.at[:, :, half], cotbuf.at[mine, own]), (gamma_hbm, gamma), (beta_hbm, beta)))]
    for c in loads:
        c.start()

    barrier = pltpu.get_barrier_semaphore()
    friends = plane + column + [partner, outer]
    for dev in friends:
        pl.semaphore_signal(barrier, inc=1, device_id=dev, device_id_type=MESH)
    pl.semaphore_wait(barrier, len(friends))

    line, there = 5 * core, 5 * (1 - core)
    loads[0].wait()
    c_act = copy(actbuf.at[:, core], actbuf.at[:, core], partner)
    loads[1].wait()
    edge_row, inner_row = 1 + 3 * core, 2 + core
    nexts, c_twin, c_next = [], [], []
    for r, dst_row in ((core, edge_row), (1 - core, inner_row)):
        slot = count[0]
        c_next.append(make(cot.at[:, r, pl.ds(0, 96)], cotbuf.at[later, dst_row], column[5], slot))
        nexts.append(c_next[-1])
        nexts.append(make(cot.at[:, r, pl.ds(96, 96)], cotbuf.at[later, dst_row], column[6], slot))

        @pl.when(u == 0)
        def _(pair_=nexts[-2:]):
            for c in pair_:
                c.start()

        c_twin.append(copy(cot.at[:, r, other_half], cotbuf.at[mine, dst_row], twin))

    c_pair = copy(cot.at[:, :, half], cotbuf.at[mine, own], partner)
    c_edge = copy(cot.at[:, core, half], cotbuf.at[mine, there], outer)

    places = ((y, yp, ym, x, xp, xm), (x, xp, xm, y, yp, ym))

    def gather_start(buf, p, plus, minus):
        return copy(buf.at[p], buf.at[p], plus), copy(buf.at[p], buf.at[p], minus)

    def gather_forward(h, buf, p, plus, minus, pair_):
        lo, hi = pl.ds(0, CUTS[h]), pl.ds(CUTS[h], LANES[h] - CUTS[h])
        pair_[0].wait_recv()
        low = lax.rem(p + 3, 4)
        f1 = copy(buf.at[low, :, lo], buf.at[low, :, lo], plus)
        pair_[1].wait_recv()
        high = lax.rem(p + 1, 4)
        f2 = copy(buf.at[high, :, hi], buf.at[high, :, hi], minus)
        return f1, f2

    first = []
    loads[2].wait()
    wide_w = w[...].astype(F32)
    wide_w = jnp.where(u == 0, wide_w[..., 0:96], wide_w[..., 96:192])
    for a in range(3):
        for b in range(9):
            k = a * TAPK + 96 * b
            wflat[0:12, k:k + 96] = wide_w[:, 9 * a + b, :]
        wflat[0:12, a * TAPK + 864:a * TAPK + TAPK] = jnp.zeros((12, 32), F32)
    for h in range(2):
        p, plus, minus = places[h][:3]
        wy[h][p] = wflat[:, 1408 * h:1408 * h + LANES[h]].astype(BF)
        first.append(gather_start(wy[h], p, plus, minus))

    for c in loads[3:]:
        c.wait()
    blk = div12(iota((192, 384), 0))
    pick = iota((192, 384), 1) == iota((192, 384), 0) + 12 * blk + 12 * core
    pick_bf = jnp.where(pick, 1.0, 0.0).astype(BF)
    gcol = jnp.sum(jnp.where(pick, gamma[...][None, :], 0.0), axis=1, keepdims=True)
    bcol = jnp.sum(jnp.where(pick, beta[...][None, :], 0.0), axis=1, keepdims=True)
    member = iota((192, 128), 1) == div12(iota((192, 128), 0))
    c_act.wait_recv()
    xt = lax.dot_general(pick_bf, actbuf[...].reshape(256, 384), (((1,), (1,)), ((), ())),
                         preferred_element_type=F32)

    def group_sums(a, b):
        lines = []
        for value in (a, b):
            for t in range(2):
                c = jnp.sum(value[:, 128 * t:128 * t + 128], axis=1, keepdims=True)
                lines.append(jnp.sum(jnp.where(member, c, 0.0), axis=0, keepdims=True))
        return jnp.concatenate(lines + [jnp.zeros((4, 128), F32)], axis=0)

    def spread(v):
        return jnp.sum(jnp.where(member, v, 0.0), axis=1, keepdims=True)

    def stats_start(k, total):
        stat_out[k] = total
        return [copy(stat_out.at[k], stat_in.at[k, d], plane[d]) for d in range(15)]

    def stats_end(k, total, cs):
        for d in range(15):
            cs[d].wait_recv()
            total = total + stat_in[k, d]
        return total

    tot1 = group_sums(xt, xt * xt)
    s1 = stats_start(0, tot1)

    def pass_edge(frames, c):
        c.wait_recv()
        return copy(cotbuf.at[frames, line], cotbuf.at[frames, line], partner)

    def pass_row(frames, r, device, to, c):
        if c is not None:
            c.wait_recv()
        return copy(cotbuf.at[frames, r], cotbuf.at[frames, to], device)

    early, late = [c_pair], []
    second = [gather_forward(h, wy[h], *places[h][:3], first[h]) for h in range(2)]
    early.append(pass_edge(mine, c_edge))
    edge1 = pass_row(theirs, edge_row, outer, there, c_twin[0])
    early.append(pass_row(theirs, edge_row, partner, edge_row, None))
    edge2 = pass_row(later, edge_row, outer, there, c_next[0])
    late.append(pass_row(later, edge_row, partner, edge_row, None))
    early.append(pass_row(theirs, inner_row, partner, inner_row, c_twin[1]))

    tot1 = stats_end(0, tot1, s1)
    mean_l = tot1[0:2] / n_norm
    inv_l = lax.rsqrt(tot1[2:4] / n_norm - mean_l * mean_l + NORM_EPS)
    wide = lambda m: jnp.concatenate(
        [jnp.broadcast_to(spread(m[t:t + 1]), (192, 128)) for t in range(2)], axis=1)
    inv = wide(inv_l)
    normed = (xt - wide(mean_l)) * inv
    shifted = normed * gcol + bcol
    gate = jax.nn.sigmoid(shifted)
    hidden = (shifted * gate).astype(BF)
    hbuf[u] = hidden
    c_hid = copy(hbuf.at[u], hbuf.at[u], twin)
    slope = gate * (1.0 + shifted * (1.0 - gate)) * gcol
    b2 = div12(iota((192, 192), 0))
    swap = iota((192, 192), 1) == iota((192, 192), 0) + 12 * ((b2 & 3) * 4 + (b2 >> 2) - b2)
    swap_bf = jnp.where(swap, 1.0, 0.0).astype(BF)
    hswap[u] = jnp.dot(swap_bf, hidden, preferred_element_type=F32).astype(BF)

    early.append(pass_edge(theirs, edge1))
    third = []
    for h in range(2):
        for f in second[h]:
            f.wait_recv()
        p2, plus2, minus2 = places[h][3:]
        parts = [wy[h][j].astype(F32)[0:12] for j in range(4)]
        wx[h][p2] = jnp.concatenate(parts, axis=0).astype(BF)
        third.append(gather_start(wx[h], p2, plus2, minus2))

    late.append(pass_row(later, inner_row, partner, inner_row, c_next[1]))
    late.append(pass_edge(later, edge2))
    for c in early:
        c.wait_recv()
    left = iota((96, 128), 1) < 64
    col, lane = iota((128, 384), 0), iota((128, 384), 1)
    shift = col - 2 * (lane & 63) + (lane >> 7) - 1
    summer = jnp.where((shift == 0) | (shift == 1), 1.0, 0.0).astype(BF)
    ghi[864:896] = jnp.zeros((32, 768), BF)
    glo[864:896] = jnp.zeros((32, 768), BF)

    def window_sums(f):
        sums = jnp.dot(cotbuf[f].reshape(576, 128), summer, preferred_element_type=F32)
        if f >= 4:
            sums = jnp.where(pair < 3, sums, 0.0)
        lines = [sums[96 * h:96 * h + 96] for h in range(6)]
        lines[0] = jnp.where(q > 0, lines[0], 0.0)
        lines[5] = jnp.where(q < 15, lines[5], 0.0)
        for e in range(3):
            ls = [v[:, 128 * e:128 * e + 128] for v in lines]
            for b in range(3):
                v = jnp.where(left, ls[2 - b] + ls[3 - b], ls[4 - b] + ls[5 - b])
                hi = v.astype(BF)
                k = (3 * b + e) * 96
                ghi[k:k + 96, 128 * f:128 * f + 128] = hi
                glo[k:k + 96, 128 * f:128 * f + 128] = (v - hi.astype(F32)).astype(BF)

    hid = (hbuf, hswap)

    def partial(n, v, first):
        for a, k0, rows, l0 in STREAM_SEGMENTS[n]:
            lanes = pl.ds(pl.multiple_of(256 * v + (2 - a) * 128, 128), 256)
            acc = None
            for g in (ghi, glo):
                d = lax.dot_general(hid[STREAMS[n][0]][v], g[k0:k0 + rows, lanes],
                                    (((1,), (1,)), ((), ())), preferred_element_type=F32)
                acc = d if acc is None else acc + d
            for j in range(4):
                if first:
                    dps[n][j, :, l0:l0 + rows] = acc[48 * j:48 * j + 48]
                else:
                    dps[n][j, :, l0:l0 + rows] += acc[48 * j:48 * j + 48]

    for f in range(4):
        window_sums(f)

    @pl.when(u == 0)
    def _():
        for n in range(4):
            partial(n, 0, True)

    for c in late:
        c.wait_recv()
    for f in range(4, 6):
        window_sums(f)

    @pl.when(u == 1)
    def _():
        for n in range(4):
            partial(n, 1, True)

    def reduce_start(n, part, sbuf, p, plus, minus, r1, r2, a_in, b_in):
        opp, nxt, prv = lax.rem(p + 2, 4), lax.rem(p + 1, 4), lax.rem(p + 3, 4)
        lo, hi = pl.ds(0, STREAMS[n][3]), pl.ds(STREAMS[n][3], STREAMS[n][2] - STREAMS[n][3])
        if sbuf is not part:
            sbuf[opp] = part[opp].astype(BF)
        o1 = copy(sbuf.at[opp, :, lo], r1, plus)
        o2 = copy(sbuf.at[opp, :, hi], r2, minus)
        if sbuf is not part:
            sbuf[nxt] = part[nxt].astype(BF)
        n1 = copy(sbuf.at[nxt, :, hi], a_in.at[:, hi], plus)
        if sbuf is not part:
            sbuf[prv] = part[prv].astype(BF)
        n2 = copy(sbuf.at[prv, :, lo], b_in.at[:, lo], minus)
        return o1, o2, n1, n2

    def reduce_mid(n, part, p, plus, minus, r1, r2, a_in, b_in, s_1, s_2, cs):
        nxt, prv = lax.rem(p + 1, 4), lax.rem(p + 3, 4)
        lo, hi = pl.ds(0, STREAMS[n][3]), pl.ds(STREAMS[n][3], STREAMS[n][2] - STREAMS[n][3])
        cs[0].wait_recv()
        s_1[...] = (part[nxt, :, lo] + r1[...].astype(F32)).astype(s_1.dtype)
        m1 = copy(s_1, a_in.at[:, lo], plus)
        cs[1].wait_recv()
        s_2[...] = (part[prv, :, hi] + r2[...].astype(F32)).astype(s_2.dtype)
        m2 = copy(s_2, b_in.at[:, hi], minus)
        return m1, m2

    def reduce_end(part, p, a_in, b_in, cs, ms):
        for c in (cs[2], cs[3], ms[0], ms[1]):
            c.wait_recv()
        return part[p] + a_in[...].astype(F32) + b_in[...].astype(F32)

    rs_places = (places[1], places[0])
    started, mids, started2, mids2 = [None] * 4, [None] * 4, [None] * 4, [None] * 4

    def first_start(n):
        p, plus, minus = rs_places[STREAMS[n][0]][:3]
        started[n] = reduce_start(n, dps[n], sbs[n], p, plus, minus,
                                  r1s[n], r2s[n], ras[n], rbs[n])

    def first_mid(n):
        p, plus, minus = rs_places[STREAMS[n][0]][:3]
        mids[n] = reduce_mid(n, dps[n], p, plus, minus, r1s[n], r2s[n], ras[n], rbs[n],
                             m1s[n], m2s[n], started[n])

    def second_start(n):
        p, _, _, p2, plus2, minus2 = rs_places[STREAMS[n][0]]
        whole = reduce_end(dps[n], p, ras[n], rbs[n], started[n], mids[n])
        for j in range(4):
            eps[n][j] = whole[12 * j:12 * j + 12]
        started2[n] = reduce_start(n, eps[n], eps[n], p2, plus2, minus2,
                                   q1s[n], q2s[n], eas[n], ecs[n])

    def second_mid(n):
        p2, plus2, minus2 = rs_places[STREAMS[n][0]][3:]
        mids2[n] = reduce_mid(n, eps[n], p2, plus2, minus2, q1s[n], q2s[n], eas[n], ecs[n],
                              t1s[n], t2s[n], started2[n])

    def pack(fin, streams):
        tops, rests = [], []
        for n in streams:
            p2 = rs_places[STREAMS[n][0]][3]
            done = reduce_end(eps[n], p2, eas[n], ecs[n], started2[n], mids2[n])
            for k in range(STREAMS[n][2] // 128):
                tops.append(done[0:8, 128 * k:128 * k + 128])
                rests.append(done[8:12, 128 * k:128 * k + 128])
        if len(rests) % 2:
            rests.append(jnp.zeros((4, 128), F32))
        tops += [jnp.concatenate(rests[2 * m:2 * m + 2], axis=0) for m in range(len(rests) // 2)]
        while len(tops) < fin.shape[0]:
            tops.append(jnp.zeros((8, 128), F32))
        for k, v in enumerate(tops):
            fin[k] = v

    def z_start(fin, zin):
        size = fin.shape[0] // 4
        return [copy(fin.at[pl.ds(size * lax.rem(pair + m, 4), size)], zin.at[m - 1],
                     column[2 * m - 1]) for m in range(1, 4)]

    def z_gather(fin, zin, zred, zout, cs):
        size = fin.shape[0] // 4
        total = fin[pl.ds(size * pair, size)]
        for m in range(3):
            cs[m].wait_recv()
            total = total + zin[m]
        total = total.reshape(size // 2, 16, 128).astype(BF)
        zred[...] = total
        place = pl.ds(size // 2 * pair, size // 2)
        gs = [copy(zred, zout.at[u, place], column[k]) for k in range(7)]
        zout[u, place] = total
        return gs

    c_hid.wait_recv()
    hswap[1 - u] = jnp.dot(swap_bf, hbuf[1 - u], preferred_element_type=F32).astype(BF)
    for n in range(4):
        partial(n, 1 - u, False)
        first_start(n)

    fourth = [gather_forward(h, wx[h], *places[h][3:], third[h]) for h in range(2)]

    for n in range(4):
        first_mid(n)
    for n in range(4):
        second_start(n)

    ag = []
    for h in range(2):
        for f in fourth[h]:
            f.wait_recv()
        acc = jnp.zeros((192, 512), F32)
        for a, k0, rows, l0 in SEGMENTS[h]:
            wa = jnp.concatenate([wx[h][j, :, l0:l0 + rows] for j in range(4)], axis=0)
            for g in (ghi, glo):
                acc = acc + jnp.dot(wa, g[k0:k0 + rows, (2 - a) * 128:(2 - a) * 128 + 512],
                                    preferred_element_type=F32)
        ag.append(acc)
    for m in range(16):
        b = (m % 4) * 4 + m // 4
        perm_scr[12 * m:12 * m + 12, :] = ag[1][12 * b:12 * b + 12]
    for v in range(2):
        actp[v] = ag[0][:, 256 * v:256 * v + 256] + perm_scr[:, 256 * v:256 * v + 256]
    c_grad = copy(actp.at[1 - u], actin, twin)

    for n in range(2):
        second_mid(n)
    for n in range(2, 4):
        second_mid(n)
    pack(fin_p, (0, 1))
    zs_p = z_start(fin_p, zin_p)
    pack(fin_q, (2, 3))
    zs_q = z_start(fin_q, zin_q)

    c_grad.wait_recv()
    norm_grad = (actp[u] + actin[...]) * slope
    tot2 = group_sums(norm_grad, norm_grad * normed)
    s2 = stats_start(1, tot2)

    zg = z_gather(fin_p, zin_p, zred_p, zout_p, zs_p)
    zg += z_gather(fin_q, zin_q, zred_q, zout_q, zs_q)
    tot2 = stats_end(1, tot2, s2)
    mean2 = tot2[0:4] / n_norm
    d = inv * (norm_grad - wide(mean2[0:2]) - normed * wide(mean2[2:4]))
    back = lax.dot_general(d.astype(BF), pick_bf, (((0,), (0,)), ((), ())),
                           preferred_element_type=F32)
    dsend[...] = back.astype(BF).reshape(2, 2, 64, 384)
    c_out = copy(dsend.at[:, 1 - core], drecv, partner)

    c_out.wait_recv()
    dacts[...] = dsend[:, core] + drecv[...]
    for c in zg:
        c.wait_recv()
    dw[:, 0:12] = zout_p[...]
    dw[:, 12:20] = zout_q[...]
    for c in copies:
        c.wait_send()

    @pl.when(u == 0)
    def _():
        for c in nexts:
            c.wait_send()


def finish(dacts_in, zout, dacts, dw, dflat):
    dacts[...] = dacts_in[...]
    for v in range(2):
        tiles = zout[v].astype(F32).reshape(40, 8, 128)
        for first, places in ((0, (0, 1, 2, 3, 4, 5, 11, 12, 13, 14, 15)),
                              (24, (6, 7, 8, 9, 10, 16, 17, 18, 19, 20))):
            for m, k in enumerate(places):
                dflat[v, 0:8, 128 * k:128 * k + 128] = tiles[first + m]
                two = tiles[first + len(places) + m // 2]
                dflat[v, 8:12, 128 * k:128 * k + 128] = two[4 * (m % 2):4 * (m % 2) + 4]
    for a in range(3):
        for b in range(9):
            k = a * TAPK + 96 * b
            dw[:, 9 * a + b, 0:96] = dflat[0, 0:12, k:k + 96]
            dw[:, 9 * a + b, 96:192] = dflat[1, 0:12, k:k + 96]


def shards(acts, gamma, beta, weights, cotangent):
    frames, low_rows, low_cols, channels = acts.shape
    n_norm = float(low_rows * 32 * low_cols * (channels // GROUPS))
    acts2 = acts.reshape(2, 64, 384)
    cot = cotangent.swapaxes(2, 3)
    vm = pl.BlockSpec(memory_space=VMEM)
    dma = pltpu.SemaphoreType.DMA((NCOPY,))
    both = lambda lead, dtype, lanes=LANES: [VMEM((*lead, n), dtype) for n in lanes]

    sizes = tuple(v[2] for v in STREAMS)
    cuts = tuple(v[3] for v in STREAMS)
    tails = tuple(n - c for n, c in zip(sizes, cuts))

    def ring(rows, dtype):
        first = both((4, rows), F32, sizes) + (both((4, rows), BF, sizes) if dtype == BF else [])
        return (first + both((rows,), dtype, cuts) + both((rows,), dtype, tails)
                + both((rows,), dtype, sizes) + both((rows,), dtype, sizes)
                + both((rows,), dtype, cuts) + both((rows,), dtype, tails))

    dacts, dw = pl.pallas_call(
        lambda *refs: kernel(n_norm, *refs),
        out_shape=(jax.ShapeDtypeStruct((2, 64, 384), BF),
                   jax.ShapeDtypeStruct((2, 20, 16, 128), BF)),
        in_specs=[pl.BlockSpec(memory_space=pltpu.HBM)] * 5,
        out_specs=(vm, vm),
        scratch_shapes=[
            VMEM((2, 2, 192, 128), BF), VMEM((12, 27, 192), BF), VMEM((384,), F32),
            VMEM((384,), F32), pltpu.SemaphoreType.DMA((6,)),
            VMEM((2, 2, 64, 384), BF), VMEM((6, 6, 96, 128), BF),
            VMEM((2, 8, 128), F32), VMEM((2, 15, 8, 128), F32),
            VMEM((TAPK, 768), BF), VMEM((TAPK, 768), BF),
            VMEM((2, 192, 256), BF), VMEM((2, 192, 256), BF),
            VMEM((16, 3 * TAPK), F32),
            *both((4, 16), BF), *both((4, 48), BF), *ring(48, BF), *ring(12, F32),
            VMEM((24, 8, 128), F32), VMEM((16, 8, 128), F32),
            VMEM((3, 6, 8, 128), F32), VMEM((3, 4, 8, 128), F32),
            VMEM((3, 16, 128), BF), VMEM((2, 16, 128), BF),
            VMEM((2, 12, 16, 128), BF), VMEM((2, 8, 16, 128), BF),
            VMEM((2, 192, 256), F32), VMEM((192, 256), F32), VMEM((192, 512), F32),
            VMEM((2, 2, 64, 384), BF), VMEM((2, 64, 384), BF),
            dma, dma,
        ],
        compiler_params=pltpu.CompilerParams(
            collective_id=0, has_side_effects=True, vmem_limit_bytes=20 * 1024 * 1024),
        name="backward",
    )(*(pltpu.with_memory_space_constraint(v, pltpu.HBM) for v in (acts2, cot, weights, gamma, beta)))
    dacts, dw = pl.pallas_call(
        finish,
        out_shape=(jax.ShapeDtypeStruct((2, 64, 384), BF),
                   jax.ShapeDtypeStruct((12, 27, 192), F32)),
        in_specs=[vm] * 2,
        out_specs=(vm, vm),
        scratch_shapes=[VMEM((2, 16, 3 * TAPK), F32)],
        compiler_params=pltpu.CompilerParams(vmem_limit_bytes=8 * 1024 * 1024),
        name="finish",
    )(dacts, dw)
    return dacts.reshape(2, 1, 64, 384), dw


def solution(mesh):
    placed = (
        P("block", "tile", None, None),
        P(),
        P(),
        P("tile", None, None),
        P("block", "tile", None, None),
    )
    return jax.shard_map(
        shards,
        mesh=mesh,
        in_specs=placed,
        out_specs=(P("block", "tile", None, None), P("tile", None, None)),
        check_vma=False,
    )
```

```python
import jax
import jax.numpy as jnp
from jax import lax
from jax.experimental import pallas as pl
from jax.experimental.pallas import tpu as pltpu
from jax.sharding import PartitionSpec as P

GROUPS = 32
NORM_EPS = 1e-06
MESH = pl.DeviceIdType.MESH
BF = jnp.bfloat16
F32 = jnp.float32
VMEM = pltpu.VMEM
NCOPY = 144
TAPK = 896
LANES = (1408, 1280)
CUTS = (768, 640)
SEGMENTS = (((0, 0, 896, 0), (1, 0, 512, 896)), ((1, 512, 384, 0), (2, 0, 896, 384)))
NARROW = (1, 2)
STREAMS = ((0, 0, 768, 384), (1, 0, 640, 384), (0, 768, 640, 384), (1, 640, 640, 384))
STREAM_SEGMENTS = (((0, 0, 768, 0),), ((1, 512, 384, 0), (2, 0, 256, 384)),
                   ((0, 768, 128, 0), (1, 0, 512, 128)), ((2, 256, 640, 0),))


def iota(shape, dim):
    return lax.broadcasted_iota(jnp.int32, shape, dim)


def div12(v):
    return (v * 5462) >> 16


def kernel(n_norm, acts, cot_hbm, w_hbm, gamma_hbm, beta_hbm, dacts, dw,
           cot, w, gamma, beta, load_sem, actbuf, cotbuf, stat_out, stat_in, ghi, glo, hbuf, hswap, wflat,
           wy0, wy1, wx0, wx1, *rest):
    dps, sbs, r1s, r2s, ras, rbs, m1s, m2s = (rest[4 * k:4 * k + 4] for k in range(8))
    eps, q1s, q2s, eas, ecs, t1s, t2s = (rest[32 + 4 * k:36 + 4 * k] for k in range(7))
    (fin_p, fin_q, zin_p, zin_q, zsend_p, zsend_q, znarrow_p, znarrow_q, zred_p, zred_q, zout_p, zout_q,
     actp, actin, perm_scr, dsend, drecv, send_sem, recv_sem) = rest[60:]
    z = lax.axis_index("block")
    tile = lax.axis_index("tile")
    core = lax.rem(tile, 2)
    q = lax.div(tile, 2)
    y = lax.rem(q, 4)
    x = lax.div(q, 4)
    u = lax.rem(z, 2)
    pair = lax.div(z, 2)
    wy, wx = (wy0, wy1), (wx0, wx1)

    def chip(cx, cy):
        return {"tile": (cx * 4 + cy) * 2 + core}

    partner = {"tile": tile + 1 - 2 * core}
    outer = {"tile": lax.rem(tile + 2 * core - 1 + 32, 32)}
    xp, xm = chip(lax.rem(x + 1, 4), y), chip(lax.rem(x + 3, 4), y)
    yp, ym = chip(x, lax.rem(y + 1, 4)), chip(x, lax.rem(y + 3, 4))
    plane = [{"tile": lax.rem(q + d, 16) * 2 + core} for d in range(1, 16)]
    column = [{"block": lax.rem(z + k, 8)} for k in range(1, 8)]
    twin = {"block": z + 1 - 2 * u}

    copies = []
    count = [0]

    def make(src, dst, device, slot=None):
        k = count[0]
        count[0] += 1
        return pltpu.make_async_remote_copy(
            src_ref=src, dst_ref=dst, send_sem=send_sem.at[k],
            recv_sem=recv_sem.at[k if slot is None else slot],
            device_id=device, device_id_type=MESH)

    def copy(src, dst, device):
        c = make(src, dst, device)
        copies.append(c)
        c.start()
        return c

    own = pl.ds(1 + 2 * core, 2)
    mine, theirs, later = pl.ds(2 * u, 2), pl.ds(2 - 2 * u, 2), pl.ds(4, 2)
    half = pl.ds(pl.multiple_of(96 * u, 32), 96)
    other_half = pl.ds(pl.multiple_of(96 - 96 * u, 32), 96)
    loads = [pltpu.make_async_copy(a, b, load_sem.at[k]) for k, (a, b) in enumerate((
        (acts, actbuf.at[:, core]), (cot_hbm, cot), (w_hbm, w),
        (cot_hbm.at[:, :, half], cotbuf.at[mine, own]), (gamma_hbm, gamma), (beta_hbm, beta)))]
    for c in loads:
        c.start()

    barrier = pltpu.get_barrier_semaphore()
    friends = plane + column + [partner, outer]
    for dev in friends:
        pl.semaphore_signal(barrier, inc=1, device_id=dev, device_id_type=MESH)
    places = ((y, yp, ym, x, xp, xm), (x, xp, xm, y, yp, ym))

    loads[2].wait()
    wide_w = w[...].astype(F32)
    wide_w = jnp.where(u == 0, wide_w[..., 0:96], wide_w[..., 96:192])
    for a in range(3):
        for b in range(9):
            k = a * TAPK + 96 * b
            wflat[0:12, k:k + 96] = wide_w[:, 9 * a + b, :]
        wflat[0:12, a * TAPK + 864:a * TAPK + TAPK] = jnp.zeros((12, 32), F32)
    for h in range(2):
        wy[h][places[h][0]] = wflat[:, 1408 * h:1408 * h + LANES[h]].astype(BF)
    for c in loads[3:] + loads[0:2]:
        c.wait()
    blk = div12(iota((192, 384), 0))
    pick = iota((192, 384), 1) == iota((192, 384), 0) + 12 * blk + 12 * core
    pick_bf = jnp.where(pick, 1.0, 0.0).astype(BF)
    gcol = jnp.sum(jnp.where(pick, gamma[...][None, :], 0.0), axis=1, keepdims=True)
    bcol = jnp.sum(jnp.where(pick, beta[...][None, :], 0.0), axis=1, keepdims=True)
    member = [iota((192, 128), 1) == div12(iota((192, 128), 0)) + 16 * k for k in range(4)]
    pl.semaphore_wait(barrier, len(friends))

    line, there = 5 * core, 5 * (1 - core)
    c_act = copy(actbuf.at[:, core], actbuf.at[:, core], partner)
    edge_row, inner_row = 1 + 3 * core, 2 + core
    nexts, c_twin, c_next = [], [], []
    for r, dst_row in ((core, edge_row), (1 - core, inner_row)):
        slot = count[0]
        c_next.append(make(cot.at[:, r, pl.ds(0, 96)], cotbuf.at[later, dst_row], column[5], slot))
        nexts.append(c_next[-1])
        nexts.append(make(cot.at[:, r, pl.ds(96, 96)], cotbuf.at[later, dst_row], column[6], slot))

        @pl.when(u == 0)
        def _(pair_=nexts[-2:]):
            for c in pair_:
                c.start()

        c_twin.append(copy(cot.at[:, r, other_half], cotbuf.at[mine, dst_row], twin))

    c_pair = copy(cot.at[:, :, half], cotbuf.at[mine, own], partner)
    c_edge = copy(cot.at[:, core, half], cotbuf.at[mine, there], outer)

    def gather_start(buf, p, plus, minus):
        return copy(buf.at[p], buf.at[p], plus), copy(buf.at[p], buf.at[p], minus)

    def gather_forward(h, buf, p, plus, minus, pair_):
        lo, hi = pl.ds(0, CUTS[h]), pl.ds(CUTS[h], LANES[h] - CUTS[h])
        pair_[0].wait_recv()
        low = lax.rem(p + 3, 4)
        f1 = copy(buf.at[low, :, lo], buf.at[low, :, lo], plus)
        pair_[1].wait_recv()
        high = lax.rem(p + 1, 4)
        f2 = copy(buf.at[high, :, hi], buf.at[high, :, hi], minus)
        return f1, f2

    first = []
    for h in range(2):
        p, plus, minus = places[h][:3]
        first.append(gather_start(wy[h], p, plus, minus))

    c_act.wait_recv()
    xt = lax.dot_general(pick_bf, actbuf[...].reshape(256, 384), (((1,), (1,)), ((), ())),
                         preferred_element_type=F32)

    def group_sums(a, b):
        total = jnp.zeros((192, 128), F32)
        for k in range(4):
            value = (a, b)[k // 2][:, 128 * (k % 2):128 * (k % 2) + 128]
            total = total + jnp.where(member[k], jnp.sum(value, axis=1, keepdims=True), 0.0)
        return jnp.sum(total, axis=0, keepdims=True)

    def spread(v, k):
        return jnp.sum(jnp.where(member[k], v, 0.0), axis=1, keepdims=True)

    def wide(first, second):
        return jnp.concatenate([jnp.broadcast_to(v, (192, 128)) for v in (first, second)], axis=1)

    def stats_start(k, total):
        stat_out[k] = total
        return [copy(stat_out.at[k], stat_in.at[k, d], plane[d]) for d in range(15)]

    def stats_end(k, total, cs):
        for d in range(15):
            cs[d].wait_recv()
            total = total + stat_in[k, d]
        return total

    tot1 = group_sums(xt, xt * xt)
    s1 = stats_start(0, tot1)

    def pass_edge(frames, c):
        c.wait_recv()
        return copy(cotbuf.at[frames, line], cotbuf.at[frames, line], partner)

    def pass_row(frames, r, device, to, c):
        if c is not None:
            c.wait_recv()
        return copy(cotbuf.at[frames, r], cotbuf.at[frames, to], device)

    early, late = [c_pair], []
    early.append(pass_edge(mine, c_edge))
    second = [gather_forward(h, wy[h], *places[h][:3], first[h]) for h in range(2)]
    edge1 = pass_row(theirs, edge_row, outer, there, c_twin[0])
    early.append(pass_row(theirs, edge_row, partner, edge_row, None))
    edge2 = pass_row(later, edge_row, outer, there, c_next[0])
    late.append(pass_row(later, edge_row, partner, edge_row, None))
    early.append(pass_row(theirs, inner_row, partner, inner_row, c_twin[1]))

    tot1 = stats_end(0, tot1, s1)
    stats = [spread(tot1, k) / n_norm for k in range(4)]
    inv = wide(*(lax.rsqrt(stats[2 + t] - stats[t] * stats[t] + NORM_EPS) for t in range(2)))
    normed = (xt - wide(*stats[0:2])) * inv
    shifted = normed * gcol + bcol
    gate = jax.nn.sigmoid(shifted)
    hidden = (shifted * gate).astype(BF)
    hbuf[u] = hidden
    c_hid = copy(hbuf.at[u], hbuf.at[u], twin)
    slope = gate * (1.0 + shifted * (1.0 - gate)) * gcol
    b2 = div12(iota((192, 192), 0))
    swap = iota((192, 192), 1) == iota((192, 192), 0) + 12 * ((b2 & 3) * 4 + (b2 >> 2) - b2)
    swap_bf = jnp.where(swap, 1.0, 0.0).astype(BF)
    hswap[u] = jnp.dot(swap_bf, hidden, preferred_element_type=F32).astype(BF)

    early.append(pass_edge(theirs, edge1))
    third = []
    for h in range(2):
        for f in second[h]:
            f.wait_recv()
        p2, plus2, minus2 = places[h][3:]
        parts = [wy[h][j].astype(F32)[0:12] for j in range(4)]
        wx[h][p2] = jnp.concatenate(parts, axis=0).astype(BF)
        third.append(gather_start(wx[h], p2, plus2, minus2))

    late.append(pass_row(later, inner_row, partner, inner_row, c_next[1]))
    late.append(pass_edge(later, edge2))
    for c in early:
        c.wait_recv()
    left = iota((96, 128), 1) < 64
    col, lane = iota((128, 384), 0), iota((128, 384), 1)
    shift = col - 2 * (lane & 63) + (lane >> 7) - 1
    summer = jnp.where((shift == 0) | (shift == 1), 1.0, 0.0).astype(BF)
    ghi[864:896] = jnp.zeros((32, 768), BF)
    glo[864:896] = jnp.zeros((32, 768), BF)

    def window_sums(f):
        sums = jnp.dot(cotbuf[f].reshape(576, 128), summer, preferred_element_type=F32)
        if f >= 4:
            sums = jnp.where(pair < 3, sums, 0.0)
        lines = [sums[96 * h:96 * h + 96] for h in range(6)]
        lines[0] = jnp.where(q > 0, lines[0], 0.0)
        lines[5] = jnp.where(q < 15, lines[5], 0.0)
        for e in range(3):
            ls = [v[:, 128 * e:128 * e + 128] for v in lines]
            for b in range(3):
                v = jnp.where(left, ls[2 - b] + ls[3 - b], ls[4 - b] + ls[5 - b])
                hi = v.astype(BF)
                k = (3 * b + e) * 96
                ghi[k:k + 96, 128 * f:128 * f + 128] = hi
                glo[k:k + 96, 128 * f:128 * f + 128] = (v - hi.astype(F32)).astype(BF)

    hid = (hbuf, hswap)

    def partial(n, v, first):
        for a, k0, rows, l0 in STREAM_SEGMENTS[n]:
            lanes = pl.ds(pl.multiple_of(256 * v + (2 - a) * 128, 128), 256)
            acc = None
            for g in (ghi, glo):
                d = lax.dot_general(hid[STREAMS[n][0]][v], g[k0:k0 + rows, lanes],
                                    (((1,), (1,)), ((), ())), preferred_element_type=F32)
                acc = d if acc is None else acc + d
            for j in range(4):
                if first:
                    dps[n][j, :, l0:l0 + rows] = acc[48 * j:48 * j + 48]
                else:
                    dps[n][j, :, l0:l0 + rows] += acc[48 * j:48 * j + 48]

    for f in range(4):
        window_sums(f)

    @pl.when(u == 0)
    def _():
        for n in range(4):
            partial(n, 0, True)

    for c in late:
        c.wait_recv()
    for f in range(4, 6):
        window_sums(f)

    @pl.when(u == 1)
    def _():
        for n in range(4):
            partial(n, 1, True)

    def reduce_start(n, part, sbuf, p, plus, minus, r1, r2, a_in, b_in):
        opp, nxt, prv = lax.rem(p + 2, 4), lax.rem(p + 1, 4), lax.rem(p + 3, 4)
        lo, hi = pl.ds(0, STREAMS[n][3]), pl.ds(STREAMS[n][3], STREAMS[n][2] - STREAMS[n][3])
        if sbuf is not part:
            sbuf[opp] = part[opp].astype(BF)
        o1 = copy(sbuf.at[opp, :, lo], r1, plus)
        o2 = copy(sbuf.at[opp, :, hi], r2, minus)
        if sbuf is not part:
            sbuf[nxt] = part[nxt].astype(BF)
        n1 = copy(sbuf.at[nxt, :, hi], a_in.at[:, hi], plus)
        if sbuf is not part:
            sbuf[prv] = part[prv].astype(BF)
        n2 = copy(sbuf.at[prv, :, lo], b_in.at[:, lo], minus)
        return o1, o2, n1, n2

    def reduce_mid(n, part, p, plus, minus, r1, r2, a_in, b_in, s_1, s_2, cs):
        nxt, prv = lax.rem(p + 1, 4), lax.rem(p + 3, 4)
        lo, hi = pl.ds(0, STREAMS[n][3]), pl.ds(STREAMS[n][3], STREAMS[n][2] - STREAMS[n][3])
        cs[0].wait_recv()
        s_1[...] = (part[nxt, :, lo] + r1[...].astype(F32)).astype(s_1.dtype)
        m1 = copy(s_1, a_in.at[:, lo], plus)
        cs[1].wait_recv()
        s_2[...] = (part[prv, :, hi] + r2[...].astype(F32)).astype(s_2.dtype)
        m2 = copy(s_2, b_in.at[:, hi], minus)
        return m1, m2

    def reduce_end(part, p, a_in, b_in, cs, ms):
        for c in (cs[2], cs[3], ms[0], ms[1]):
            c.wait_recv()
        return part[p] + a_in[...].astype(F32) + b_in[...].astype(F32)

    rs_places = (places[1], places[0])
    started, mids, started2, mids2 = [None] * 4, [None] * 4, [None] * 4, [None] * 4

    def first_start(n):
        p, plus, minus = rs_places[STREAMS[n][0]][:3]
        started[n] = reduce_start(n, dps[n], sbs[n], p, plus, minus,
                                  r1s[n], r2s[n], ras[n], rbs[n])

    def first_mid(n):
        p, plus, minus = rs_places[STREAMS[n][0]][:3]
        mids[n] = reduce_mid(n, dps[n], p, plus, minus, r1s[n], r2s[n], ras[n], rbs[n],
                             m1s[n], m2s[n], started[n])

    def second_start(n):
        p, _, _, p2, plus2, minus2 = rs_places[STREAMS[n][0]]
        whole = reduce_end(dps[n], p, ras[n], rbs[n], started[n], mids[n])
        for j in range(4):
            eps[n][j] = whole[12 * j:12 * j + 12]
        started2[n] = reduce_start(n, eps[n], eps[n], p2, plus2, minus2,
                                   q1s[n], q2s[n], eas[n], ecs[n])

    def second_mid(n):
        p2, plus2, minus2 = rs_places[STREAMS[n][0]][3:]
        mids2[n] = reduce_mid(n, eps[n], p2, plus2, minus2, q1s[n], q2s[n], eas[n], ecs[n],
                              t1s[n], t2s[n], started2[n])

    def pack(fin, streams):
        tops, rests = [], []
        for n in streams:
            p2 = rs_places[STREAMS[n][0]][3]
            done = reduce_end(eps[n], p2, eas[n], ecs[n], started2[n], mids2[n])
            for k in range(STREAMS[n][2] // 128):
                tops.append(done[0:8, 128 * k:128 * k + 128])
                rests.append(done[8:12, 128 * k:128 * k + 128])
        if len(rests) % 2:
            rests.append(jnp.zeros((4, 128), F32))
        tops += [jnp.concatenate(rests[2 * m:2 * m + 2], axis=0) for m in range(len(rests) // 2)]
        while len(tops) < fin.shape[0]:
            tops.append(jnp.zeros((8, 128), F32))
        for k, v in enumerate(tops):
            fin[k] = v

    def z_start(fin, zin, zsend, znarrow):
        size = fin.shape[0] // 4
        cs = []
        for m in (2, 1, 3):
            place = pl.ds(size * lax.rem(pair + m, 4), size)
            if m in NARROW:
                zsend[m - 1] = fin[place].astype(BF)
                cs.append(copy(zsend.at[m - 1], znarrow.at[m - 1], column[2 * m - 1]))
            else:
                cs.append(copy(fin.at[place], zin.at[m - 1], column[2 * m - 1]))
        return cs

    def z_gather(fin, zin, znarrow, zred, zout, cs):
        size = fin.shape[0] // 4
        total = fin[pl.ds(size * pair, size)]
        for m, c in zip((2, 1, 3), cs):
            c.wait_recv()
            if m in NARROW:
                total = total + znarrow[m - 1].astype(F32)
            else:
                total = total + zin[m - 1]
        total = total.astype(BF)
        zred[...] = total
        place = pl.ds(size * pair, size)
        gs = [copy(zred, zout.at[u, place], column[k]) for k in (3, 2, 4, 1, 5, 0, 6)]
        zout[u, place] = total
        return gs

    c_hid.wait_recv()
    hswap[1 - u] = jnp.dot(swap_bf, hbuf[1 - u], preferred_element_type=F32).astype(BF)
    for n in range(4):
        partial(n, 1 - u, False)
        first_start(n)

    fourth = [gather_forward(h, wx[h], *places[h][3:], third[h]) for h in range(2)]

    for n in range(4):
        first_mid(n)
    for n in range(4):
        second_start(n)

    ag = []
    for h in range(2):
        for f in fourth[h]:
            f.wait_recv()
        acc = jnp.zeros((192, 512), F32)
        for a, k0, rows, l0 in SEGMENTS[h]:
            wa = jnp.concatenate([wx[h][j, :, l0:l0 + rows] for j in range(4)], axis=0)
            for g in (ghi, glo):
                acc = acc + jnp.dot(wa, g[k0:k0 + rows, (2 - a) * 128:(2 - a) * 128 + 512],
                                    preferred_element_type=F32)
        ag.append(acc)
    for m in range(16):
        b = (m % 4) * 4 + m // 4
        perm_scr[12 * m:12 * m + 12, :] = ag[1][12 * b:12 * b + 12]
    for v in range(2):
        actp[v] = ag[0][:, 256 * v:256 * v + 256] + perm_scr[:, 256 * v:256 * v + 256]
    c_grad = copy(actp.at[1 - u], actin, twin)

    for n in range(2):
        second_mid(n)
    for n in range(2, 4):
        second_mid(n)
    pack(fin_p, (0, 1))
    zs_p = z_start(fin_p, zin_p, zsend_p, znarrow_p)
    pack(fin_q, (2, 3))
    zs_q = z_start(fin_q, zin_q, zsend_q, znarrow_q)

    c_grad.wait_recv()
    norm_grad = (actp[u] + actin[...]) * slope
    tot2 = group_sums(norm_grad, norm_grad * normed)
    s2 = stats_start(1, tot2)

    zg = z_gather(fin_p, zin_p, znarrow_p, zred_p, zout_p, zs_p)
    zg += z_gather(fin_q, zin_q, znarrow_q, zred_q, zout_q, zs_q)
    tot2 = stats_end(1, tot2, s2)
    mean2 = [spread(tot2, k) / n_norm for k in range(4)]
    d = inv * (norm_grad - wide(*mean2[0:2]) - normed * wide(*mean2[2:4]))
    back = lax.dot_general(d.astype(BF), pick_bf, (((0,), (0,)), ((), ())),
                           preferred_element_type=F32)
    dsend[...] = back.astype(BF).reshape(2, 2, 64, 384)
    c_out = copy(dsend.at[:, 1 - core], drecv, partner)

    c_out.wait_recv()
    dacts[...] = dsend[:, core] + drecv[...]
    for c in zg:
        c.wait_recv()
    dw[:, 0:20] = zout_p[...]
    dw[:, 20:36] = zout_q[...]
    for c in copies:
        c.wait_send()

    @pl.when(u == 0)
    def _():
        for c in nexts:
            c.wait_send()


def finish(dacts_in, zout, dacts, dw, dflat):
    dacts[...] = dacts_in[...]
    for v in range(2):
        tiles = zout[v].astype(F32)
        for first, places in ((0, (0, 1, 2, 3, 4, 5, 11, 12, 13, 14, 15)),
                              (20, (6, 7, 8, 9, 10, 16, 17, 18, 19, 20))):
            for m, k in enumerate(places):
                dflat[v, 0:8, 128 * k:128 * k + 128] = tiles[first + m]
                two = tiles[first + len(places) + m // 2]
                dflat[v, 8:12, 128 * k:128 * k + 128] = two[4 * (m % 2):4 * (m % 2) + 4]
    for a in range(3):
        for b in range(9):
            k = a * TAPK + 96 * b
            dw[:, 9 * a + b, 0:96] = dflat[0, 0:12, k:k + 96]
            dw[:, 9 * a + b, 96:192] = dflat[1, 0:12, k:k + 96]


def shards(acts, gamma, beta, weights, cotangent):
    frames, low_rows, low_cols, channels = acts.shape
    n_norm = float(low_rows * 32 * low_cols * (channels // GROUPS))
    acts2 = acts.reshape(2, 64, 384)
    cot = cotangent.swapaxes(2, 3)
    vm = pl.BlockSpec(memory_space=VMEM)
    dma = pltpu.SemaphoreType.DMA((NCOPY,))
    both = lambda lead, dtype, lanes=LANES: [VMEM((*lead, n), dtype) for n in lanes]

    sizes = tuple(v[2] for v in STREAMS)
    cuts = tuple(v[3] for v in STREAMS)
    tails = tuple(n - c for n, c in zip(sizes, cuts))

    def ring(rows, dtype):
        first = both((4, rows), F32, sizes) + (both((4, rows), BF, sizes) if dtype == BF else [])
        return (first + both((rows,), dtype, cuts) + both((rows,), dtype, tails)
                + both((rows,), dtype, sizes) + both((rows,), dtype, sizes)
                + both((rows,), dtype, cuts) + both((rows,), dtype, tails))

    dacts, dw = pl.pallas_call(
        lambda *refs: kernel(n_norm, *refs),
        out_shape=(jax.ShapeDtypeStruct((2, 64, 384), BF),
                   jax.ShapeDtypeStruct((2, 36, 8, 128), BF)),
        in_specs=[pl.BlockSpec(memory_space=pltpu.HBM)] * 5,
        out_specs=(vm, vm),
        scratch_shapes=[
            VMEM((2, 2, 192, 128), BF), VMEM((12, 27, 192), BF), VMEM((384,), F32),
            VMEM((384,), F32), pltpu.SemaphoreType.DMA((6,)),
            VMEM((2, 2, 64, 384), BF), VMEM((6, 6, 96, 128), BF),
            VMEM((2, 1, 128), F32), VMEM((2, 15, 1, 128), F32),
            VMEM((TAPK, 768), BF), VMEM((TAPK, 768), BF),
            VMEM((2, 192, 256), BF), VMEM((2, 192, 256), BF),
            VMEM((16, 3 * TAPK), F32),
            *both((4, 16), BF), *both((4, 48), BF), *ring(48, BF), *ring(12, F32),
            VMEM((20, 8, 128), F32), VMEM((16, 8, 128), F32),
            VMEM((3, 5, 8, 128), F32), VMEM((3, 4, 8, 128), F32),
            VMEM((3, 5, 8, 128), BF), VMEM((3, 4, 8, 128), BF),
            VMEM((3, 5, 8, 128), BF), VMEM((3, 4, 8, 128), BF),
            VMEM((5, 8, 128), BF), VMEM((4, 8, 128), BF),
            VMEM((2, 20, 8, 128), BF), VMEM((2, 16, 8, 128), BF),
            VMEM((2, 192, 256), F32), VMEM((192, 256), F32), VMEM((192, 512), F32),
            VMEM((2, 2, 64, 384), BF), VMEM((2, 64, 384), BF),
            dma, dma,
        ],
        compiler_params=pltpu.CompilerParams(
            collective_id=0, has_side_effects=True, vmem_limit_bytes=20 * 1024 * 1024),
        name="backward",
    )(*(pltpu.with_memory_space_constraint(v, pltpu.HBM) for v in (acts2, cot, weights, gamma, beta)))
    dacts, dw = pl.pallas_call(
        finish,
        out_shape=(jax.ShapeDtypeStruct((2, 64, 384), BF),
                   jax.ShapeDtypeStruct((12, 27, 192), F32)),
        in_specs=[vm] * 2,
        out_specs=(vm, vm),
        scratch_shapes=[VMEM((2, 16, 3 * TAPK), F32)],
        compiler_params=pltpu.CompilerParams(vmem_limit_bytes=8 * 1024 * 1024),
        name="finish",
    )(dacts, dw)
    return dacts.reshape(2, 1, 64, 384), dw


def solution(mesh):
    placed = (
        P("block", "tile", None, None),
        P(),
        P(),
        P("tile", None, None),
        P("block", "tile", None, None),
    )
    return jax.shard_map(
        shards,
        mesh=mesh,
        in_specs=placed,
        out_specs=(P("block", "tile", None, None), P("tile", None, None)),
        check_vma=False,
    )
```

```python
import jax
import jax.numpy as jnp
from jax import lax
from jax.experimental import pallas as pl
from jax.experimental.pallas import tpu as pltpu
from jax.sharding import PartitionSpec as P

GROUPS = 32
NORM_EPS = 1e-06
MESH = pl.DeviceIdType.MESH
BF = jnp.bfloat16
F32 = jnp.float32
VMEM = pltpu.VMEM
NCOPY = 144
TAPK = 896
LANES = (1408, 1280)
CUTS = (768, 640)
SEGMENTS = (((0, 0, 896, 0), (1, 0, 512, 896)), ((1, 512, 384, 0), (2, 0, 896, 384)))
NARROW = (1, 2, 3)
STREAMS = ((0, 0, 768, 384), (1, 0, 640, 384), (0, 768, 640, 384), (1, 640, 640, 384))
STREAM_SEGMENTS = (((0, 0, 768, 0),), ((1, 512, 384, 0), (2, 0, 256, 384)),
                   ((0, 768, 128, 0), (1, 0, 512, 128)), ((2, 256, 640, 0),))


def iota(shape, dim):
    return lax.broadcasted_iota(jnp.int32, shape, dim)


def div12(v):
    return (v * 5462) >> 16


def kernel(n_norm, acts, cot_hbm, w_hbm, gamma_hbm, beta_hbm, dacts, dw,
           cot, w, gamma, beta, load_sem, actbuf, cotbuf, stat_out, stat_in, ghi, glo, hbuf, hswap, wflat,
           wy0, wy1, wx0, wx1, *rest):
    dps, sbs, r1s, r2s, ras, rbs, m1s, m2s = (rest[4 * k:4 * k + 4] for k in range(8))
    eps, q1s, q2s, eas, ecs, t1s, t2s = (rest[32 + 4 * k:36 + 4 * k] for k in range(7))
    (fin_p, fin_q, zin_p, zin_q, zsend_p, zsend_q, znarrow_p, znarrow_q, zred_p, zred_q, zout_p, zout_q,
     actp, actin, perm_scr, dsend, drecv, send_sem, recv_sem) = rest[60:]
    z = lax.axis_index("block")
    tile = lax.axis_index("tile")
    core = lax.rem(tile, 2)
    q = lax.div(tile, 2)
    y = lax.rem(q, 4)
    x = lax.div(q, 4)
    u = lax.rem(z, 2)
    pair = lax.div(z, 2)
    wy, wx = (wy0, wy1), (wx0, wx1)

    def chip(cx, cy):
        return {"tile": (cx * 4 + cy) * 2 + core}

    partner = {"tile": tile + 1 - 2 * core}
    outer = {"tile": lax.rem(tile + 2 * core - 1 + 32, 32)}
    xp, xm = chip(lax.rem(x + 1, 4), y), chip(lax.rem(x + 3, 4), y)
    yp, ym = chip(x, lax.rem(y + 1, 4)), chip(x, lax.rem(y + 3, 4))
    plane = [{"tile": lax.rem(q + d, 16) * 2 + core} for d in range(1, 16)]
    column = [{"block": lax.rem(z + k, 8)} for k in range(1, 8)]
    twin = {"block": z + 1 - 2 * u}

    copies = []
    count = [0]

    def make(src, dst, device, slot=None):
        k = count[0]
        count[0] += 1
        return pltpu.make_async_remote_copy(
            src_ref=src, dst_ref=dst, send_sem=send_sem.at[k],
            recv_sem=recv_sem.at[k if slot is None else slot],
            device_id=device, device_id_type=MESH)

    def copy(src, dst, device):
        c = make(src, dst, device)
        copies.append(c)
        c.start()
        return c

    own = pl.ds(1 + 2 * core, 2)
    mine, theirs, later = pl.ds(2 * u, 2), pl.ds(2 - 2 * u, 2), pl.ds(4, 2)
    half = pl.ds(pl.multiple_of(96 * u, 32), 96)
    other_half = pl.ds(pl.multiple_of(96 - 96 * u, 32), 96)
    loads = [pltpu.make_async_copy(a, b, load_sem.at[k]) for k, (a, b) in enumerate((
        (acts, actbuf.at[:, core]), (cot_hbm, cot), (w_hbm, w),
        (cot_hbm.at[:, :, half], cotbuf.at[mine, own]), (gamma_hbm, gamma), (beta_hbm, beta)))]
    for c in loads:
        c.start()

    barrier = pltpu.get_barrier_semaphore()
    friends = plane + column + [partner, outer]
    for dev in friends:
        pl.semaphore_signal(barrier, inc=1, device_id=dev, device_id_type=MESH)
    places = ((y, yp, ym, x, xp, xm), (x, xp, xm, y, yp, ym))

    loads[2].wait()
    wide_w = w[...].astype(F32)
    wide_w = jnp.where(u == 0, wide_w[..., 0:96], wide_w[..., 96:192])
    for a in range(3):
        for b in range(9):
            k = a * TAPK + 96 * b
            wflat[0:12, k:k + 96] = wide_w[:, 9 * a + b, :]
        wflat[0:12, a * TAPK + 864:a * TAPK + TAPK] = jnp.zeros((12, 32), F32)
    for h in range(2):
        wy[h][places[h][0]] = wflat[:, 1408 * h:1408 * h + LANES[h]].astype(BF)
    for c in loads[3:] + loads[0:2]:
        c.wait()
    blk = div12(iota((192, 384), 0))
    pick = iota((192, 384), 1) == iota((192, 384), 0) + 12 * blk + 12 * core
    pick_bf = jnp.where(pick, 1.0, 0.0).astype(BF)
    gcol = jnp.sum(jnp.where(pick, gamma[...][None, :], 0.0), axis=1, keepdims=True)
    bcol = jnp.sum(jnp.where(pick, beta[...][None, :], 0.0), axis=1, keepdims=True)
    member = [iota((192, 128), 1) == div12(iota((192, 128), 0)) + 16 * k for k in range(4)]
    pl.semaphore_wait(barrier, len(friends))

    line, there = 5 * core, 5 * (1 - core)
    c_act = copy(actbuf.at[:, core], actbuf.at[:, core], partner)
    edge_row, inner_row = 1 + 3 * core, 2 + core
    nexts, c_twin, c_next = [], [], []
    for r, dst_row in ((core, edge_row), (1 - core, inner_row)):
        slot = count[0]
        c_next.append(make(cot.at[:, r, pl.ds(0, 96)], cotbuf.at[later, dst_row], column[5], slot))
        nexts.append(c_next[-1])
        nexts.append(make(cot.at[:, r, pl.ds(96, 96)], cotbuf.at[later, dst_row], column[6], slot))

        @pl.when(u == 0)
        def _(pair_=nexts[-2:]):
            for c in pair_:
                c.start()

        c_twin.append(copy(cot.at[:, r, other_half], cotbuf.at[mine, dst_row], twin))

    c_pair = copy(cot.at[:, :, half], cotbuf.at[mine, own], partner)
    c_edge = copy(cot.at[:, core, half], cotbuf.at[mine, there], outer)

    def gather_start(buf, p, plus, minus):
        return copy(buf.at[p], buf.at[p], plus), copy(buf.at[p], buf.at[p], minus)

    def gather_forward(h, buf, p, plus, minus, pair_):
        lo, hi = pl.ds(0, CUTS[h]), pl.ds(CUTS[h], LANES[h] - CUTS[h])
        pair_[0].wait_recv()
        low = lax.rem(p + 3, 4)
        f1 = copy(buf.at[low, :, lo], buf.at[low, :, lo], plus)
        pair_[1].wait_recv()
        high = lax.rem(p + 1, 4)
        f2 = copy(buf.at[high, :, hi], buf.at[high, :, hi], minus)
        return f1, f2

    first = []
    for h in range(2):
        p, plus, minus = places[h][:3]
        first.append(gather_start(wy[h], p, plus, minus))

    c_act.wait_recv()
    xt = lax.dot_general(pick_bf, actbuf[...].reshape(256, 384), (((1,), (1,)), ((), ())),
                         preferred_element_type=F32)

    def group_sums(a, b):
        total = jnp.zeros((192, 128), F32)
        for k in range(4):
            value = (a, b)[k // 2][:, 128 * (k % 2):128 * (k % 2) + 128]
            total = total + jnp.where(member[k], jnp.sum(value, axis=1, keepdims=True), 0.0)
        return jnp.sum(total, axis=0, keepdims=True)

    def spread(v, k):
        return jnp.sum(jnp.where(member[k], v, 0.0), axis=1, keepdims=True)

    def wide(first, second):
        return jnp.concatenate([jnp.broadcast_to(v, (192, 128)) for v in (first, second)], axis=1)

    def stats_start(k, total):
        stat_out[k] = total
        return [copy(stat_out.at[k], stat_in.at[k, d], plane[d]) for d in range(15)]

    def stats_end(k, total, cs):
        for d in range(15):
            cs[d].wait_recv()
            total = total + stat_in[k, d]
        return total

    tot1 = group_sums(xt, xt * xt)
    s1 = stats_start(0, tot1)

    def pass_edge(frames, c):
        c.wait_recv()
        return copy(cotbuf.at[frames, line], cotbuf.at[frames, line], partner)

    def pass_row(frames, r, device, to, c):
        if c is not None:
            c.wait_recv()
        return copy(cotbuf.at[frames, r], cotbuf.at[frames, to], device)

    early, late = [c_pair], []
    early.append(pass_edge(mine, c_edge))
    second = [gather_forward(h, wy[h], *places[h][:3], first[h]) for h in range(2)]
    edge1 = pass_row(theirs, edge_row, outer, there, c_twin[0])
    early.append(pass_row(theirs, edge_row, partner, edge_row, None))
    edge2 = pass_row(later, edge_row, outer, there, c_next[0])
    late.append(pass_row(later, edge_row, partner, edge_row, None))
    early.append(pass_row(theirs, inner_row, partner, inner_row, c_twin[1]))

    tot1 = stats_end(0, tot1, s1)
    stats = [spread(tot1, k) / n_norm for k in range(4)]
    inv = wide(*(lax.rsqrt(stats[2 + t] - stats[t] * stats[t] + NORM_EPS) for t in range(2)))
    normed = (xt - wide(*stats[0:2])) * inv
    shifted = normed * gcol + bcol
    gate = jax.nn.sigmoid(shifted)
    hidden = (shifted * gate).astype(BF)
    hbuf[u] = hidden
    c_hid = copy(hbuf.at[u], hbuf.at[u], twin)
    slope = gate * (1.0 + shifted * (1.0 - gate)) * gcol
    b2 = div12(iota((192, 192), 0))
    swap = iota((192, 192), 1) == iota((192, 192), 0) + 12 * ((b2 & 3) * 4 + (b2 >> 2) - b2)
    swap_bf = jnp.where(swap, 1.0, 0.0).astype(BF)
    hswap[u] = jnp.dot(swap_bf, hidden, preferred_element_type=F32).astype(BF)

    early.append(pass_edge(theirs, edge1))
    third = []
    for h in range(2):
        for f in second[h]:
            f.wait_recv()
        p2, plus2, minus2 = places[h][3:]
        parts = [wy[h][j].astype(F32)[0:12] for j in range(4)]
        wx[h][p2] = jnp.concatenate(parts, axis=0).astype(BF)
        third.append(gather_start(wx[h], p2, plus2, minus2))

    late.append(pass_row(later, inner_row, partner, inner_row, c_next[1]))
    late.append(pass_edge(later, edge2))
    for c in early:
        c.wait_recv()
    left = iota((96, 128), 1) < 64
    col, lane = iota((128, 384), 0), iota((128, 384), 1)
    shift = col - 2 * (lane & 63) + (lane >> 7) - 1
    summer = jnp.where((shift == 0) | (shift == 1), 1.0, 0.0).astype(BF)
    ghi[864:896] = jnp.zeros((32, 768), BF)
    glo[864:896] = jnp.zeros((32, 768), BF)

    def window_sums(f):
        sums = jnp.dot(cotbuf[f].reshape(576, 128), summer, preferred_element_type=F32)
        if f >= 4:
            sums = jnp.where(pair < 3, sums, 0.0)
        lines = [sums[96 * h:96 * h + 96] for h in range(6)]
        lines[0] = jnp.where(q > 0, lines[0], 0.0)
        lines[5] = jnp.where(q < 15, lines[5], 0.0)
        for e in range(3):
            ls = [v[:, 128 * e:128 * e + 128] for v in lines]
            for b in range(3):
                v = jnp.where(left, ls[2 - b] + ls[3 - b], ls[4 - b] + ls[5 - b])
                hi = v.astype(BF)
                k = (3 * b + e) * 96
                ghi[k:k + 96, 128 * f:128 * f + 128] = hi
                glo[k:k + 96, 128 * f:128 * f + 128] = (v - hi.astype(F32)).astype(BF)

    hid = (hbuf, hswap)

    def partial(n, v, first):
        for a, k0, rows, l0 in STREAM_SEGMENTS[n]:
            lanes = pl.ds(pl.multiple_of(256 * v + (2 - a) * 128, 128), 256)
            acc = None
            for g in (ghi, glo):
                d = lax.dot_general(hid[STREAMS[n][0]][v], g[k0:k0 + rows, lanes],
                                    (((1,), (1,)), ((), ())), preferred_element_type=F32)
                acc = d if acc is None else acc + d
            for j in range(4):
                if first:
                    dps[n][j, :, l0:l0 + rows] = acc[48 * j:48 * j + 48]
                else:
                    dps[n][j, :, l0:l0 + rows] += acc[48 * j:48 * j + 48]

    for f in range(4):
        window_sums(f)

    @pl.when(u == 0)
    def _():
        for n in range(4):
            partial(n, 0, True)

    for c in late:
        c.wait_recv()
    for f in range(4, 6):
        window_sums(f)

    @pl.when(u == 1)
    def _():
        for n in range(4):
            partial(n, 1, True)

    def reduce_start(n, part, sbuf, p, plus, minus, r1, r2, a_in, b_in):
        opp, nxt, prv = lax.rem(p + 2, 4), lax.rem(p + 1, 4), lax.rem(p + 3, 4)
        lo, hi = pl.ds(0, STREAMS[n][3]), pl.ds(STREAMS[n][3], STREAMS[n][2] - STREAMS[n][3])
        if sbuf is not part:
            sbuf[opp] = part[opp].astype(BF)
        o1 = copy(sbuf.at[opp, :, lo], r1, plus)
        o2 = copy(sbuf.at[opp, :, hi], r2, minus)
        if sbuf is not part:
            sbuf[nxt] = part[nxt].astype(BF)
        n1 = copy(sbuf.at[nxt, :, hi], a_in.at[:, hi], plus)
        if sbuf is not part:
            sbuf[prv] = part[prv].astype(BF)
        n2 = copy(sbuf.at[prv, :, lo], b_in.at[:, lo], minus)
        return o1, o2, n1, n2

    def reduce_mid(n, part, p, plus, minus, r1, r2, a_in, b_in, s_1, s_2, cs):
        nxt, prv = lax.rem(p + 1, 4), lax.rem(p + 3, 4)
        lo, hi = pl.ds(0, STREAMS[n][3]), pl.ds(STREAMS[n][3], STREAMS[n][2] - STREAMS[n][3])
        cs[0].wait_recv()
        s_1[...] = (part[nxt, :, lo] + r1[...].astype(F32)).astype(s_1.dtype)
        m1 = copy(s_1, a_in.at[:, lo], plus)
        cs[1].wait_recv()
        s_2[...] = (part[prv, :, hi] + r2[...].astype(F32)).astype(s_2.dtype)
        m2 = copy(s_2, b_in.at[:, hi], minus)
        return m1, m2

    def reduce_end(part, p, a_in, b_in, cs, ms):
        for c in (cs[2], cs[3], ms[0], ms[1]):
            c.wait_recv()
        return part[p] + a_in[...].astype(F32) + b_in[...].astype(F32)

    rs_places = (places[1], places[0])
    started, mids, started2, mids2 = [None] * 4, [None] * 4, [None] * 4, [None] * 4

    def first_start(n):
        p, plus, minus = rs_places[STREAMS[n][0]][:3]
        started[n] = reduce_start(n, dps[n], sbs[n], p, plus, minus,
                                  r1s[n], r2s[n], ras[n], rbs[n])

    def first_mid(n):
        p, plus, minus = rs_places[STREAMS[n][0]][:3]
        mids[n] = reduce_mid(n, dps[n], p, plus, minus, r1s[n], r2s[n], ras[n], rbs[n],
                             m1s[n], m2s[n], started[n])

    def second_start(n):
        p, _, _, p2, plus2, minus2 = rs_places[STREAMS[n][0]]
        whole = reduce_end(dps[n], p, ras[n], rbs[n], started[n], mids[n])
        for j in range(4):
            eps[n][j] = whole[12 * j:12 * j + 12]
        started2[n] = reduce_start(n, eps[n], eps[n], p2, plus2, minus2,
                                   q1s[n], q2s[n], eas[n], ecs[n])

    def second_mid(n):
        p2, plus2, minus2 = rs_places[STREAMS[n][0]][3:]
        mids2[n] = reduce_mid(n, eps[n], p2, plus2, minus2, q1s[n], q2s[n], eas[n], ecs[n],
                              t1s[n], t2s[n], started2[n])

    def pack(fin, streams):
        tops, rests = [], []
        for n in streams:
            p2 = rs_places[STREAMS[n][0]][3]
            done = reduce_end(eps[n], p2, eas[n], ecs[n], started2[n], mids2[n])
            for k in range(STREAMS[n][2] // 128):
                tops.append(done[0:8, 128 * k:128 * k + 128])
                rests.append(done[8:12, 128 * k:128 * k + 128])
        if len(rests) % 2:
            rests.append(jnp.zeros((4, 128), F32))
        tops += [jnp.concatenate(rests[2 * m:2 * m + 2], axis=0) for m in range(len(rests) // 2)]
        while len(tops) < fin.shape[0]:
            tops.append(jnp.zeros((8, 128), F32))
        for k, v in enumerate(tops):
            fin[k] = v

    def z_start(fin, zin, zsend, znarrow):
        size = fin.shape[0] // 4
        cs = []
        for m in (2, 1, 3):
            place = pl.ds(size * lax.rem(pair + m, 4), size)
            if m in NARROW:
                zsend[m - 1] = fin[place].astype(BF)
                cs.append(copy(zsend.at[m - 1], znarrow.at[m - 1], column[2 * m - 1]))
            else:
                cs.append(copy(fin.at[place], zin.at[m - 1], column[2 * m - 1]))
        return cs

    def z_gather(fin, zin, znarrow, zred, zout, cs):
        size = fin.shape[0] // 4
        total = fin[pl.ds(size * pair, size)]
        for m, c in zip((2, 1, 3), cs):
            c.wait_recv()
            if m in NARROW:
                total = total + znarrow[m - 1].astype(F32)
            else:
                total = total + zin[m - 1]
        total = total.astype(BF)
        zred[...] = total
        place = pl.ds(size * pair, size)
        gs = [copy(zred, zout.at[u, place], column[k]) for k in (3, 2, 4, 1, 5, 0, 6)]
        zout[u, place] = total
        return gs

    c_hid.wait_recv()
    hswap[1 - u] = jnp.dot(swap_bf, hbuf[1 - u], preferred_element_type=F32).astype(BF)
    for n in range(4):
        partial(n, 1 - u, False)
        first_start(n)

    fourth = [gather_forward(h, wx[h], *places[h][3:], third[h]) for h in range(2)]

    for n in range(4):
        first_mid(n)
    for n in range(4):
        second_start(n)

    ag = []
    for h in range(2):
        for f in fourth[h]:
            f.wait_recv()
        acc = jnp.zeros((192, 512), F32)
        for a, k0, rows, l0 in SEGMENTS[h]:
            wa = jnp.concatenate([wx[h][j, :, l0:l0 + rows] for j in range(4)], axis=0)
            for g in (ghi, glo):
                acc = acc + jnp.dot(wa, g[k0:k0 + rows, (2 - a) * 128:(2 - a) * 128 + 512],
                                    preferred_element_type=F32)
        ag.append(acc)
    for m in range(16):
        b = (m % 4) * 4 + m // 4
        perm_scr[12 * m:12 * m + 12, :] = ag[1][12 * b:12 * b + 12]
    for v in range(2):
        actp[v] = ag[0][:, 256 * v:256 * v + 256] + perm_scr[:, 256 * v:256 * v + 256]
    c_grad = copy(actp.at[1 - u], actin, twin)

    for n in range(2):
        second_mid(n)
    for n in range(2, 4):
        second_mid(n)
    pack(fin_p, (0, 1))
    zs_p = z_start(fin_p, zin_p, zsend_p, znarrow_p)
    pack(fin_q, (2, 3))
    zs_q = z_start(fin_q, zin_q, zsend_q, znarrow_q)

    c_grad.wait_recv()
    norm_grad = (actp[u] + actin[...]) * slope
    tot2 = group_sums(norm_grad, norm_grad * normed)
    s2 = stats_start(1, tot2)

    zg = z_gather(fin_p, zin_p, znarrow_p, zred_p, zout_p, zs_p)
    zg += z_gather(fin_q, zin_q, znarrow_q, zred_q, zout_q, zs_q)
    tot2 = stats_end(1, tot2, s2)
    mean2 = [spread(tot2, k) / n_norm for k in range(4)]
    d = inv * (norm_grad - wide(*mean2[0:2]) - normed * wide(*mean2[2:4]))
    back = lax.dot_general(d.astype(BF), pick_bf, (((0,), (0,)), ((), ())),
                           preferred_element_type=F32)
    dsend[...] = back.astype(BF).reshape(2, 2, 64, 384)
    c_out = copy(dsend.at[:, 1 - core], drecv, partner)

    c_out.wait_recv()
    dacts[...] = dsend[:, core] + drecv[...]
    for c in zg:
        c.wait_recv()
    dw[:, 0:20] = zout_p[...]
    dw[:, 20:36] = zout_q[...]
    for c in copies:
        c.wait_send()

    @pl.when(u == 0)
    def _():
        for c in nexts:
            c.wait_send()


def finish(dacts_in, zout, dacts, dw, dflat):
    dacts[...] = dacts_in[...]
    for v in range(2):
        tiles = zout[v].astype(F32)
        for first, places in ((0, (0, 1, 2, 3, 4, 5, 11, 12, 13, 14, 15)),
                              (20, (6, 7, 8, 9, 10, 16, 17, 18, 19, 20))):
            for m, k in enumerate(places):
                dflat[v, 0:8, 128 * k:128 * k + 128] = tiles[first + m]
                two = tiles[first + len(places) + m // 2]
                dflat[v, 8:12, 128 * k:128 * k + 128] = two[4 * (m % 2):4 * (m % 2) + 4]
    for a in range(3):
        for b in range(9):
            k = a * TAPK + 96 * b
            dw[:, 9 * a + b, 0:96] = dflat[0, 0:12, k:k + 96]
            dw[:, 9 * a + b, 96:192] = dflat[1, 0:12, k:k + 96]


def shards(acts, gamma, beta, weights, cotangent):
    frames, low_rows, low_cols, channels = acts.shape
    n_norm = float(low_rows * 32 * low_cols * (channels // GROUPS))
    acts2 = acts.reshape(2, 64, 384)
    cot = cotangent.swapaxes(2, 3)
    vm = pl.BlockSpec(memory_space=VMEM)
    dma = pltpu.SemaphoreType.DMA((NCOPY,))
    both = lambda lead, dtype, lanes=LANES: [VMEM((*lead, n), dtype) for n in lanes]

    sizes = tuple(v[2] for v in STREAMS)
    cuts = tuple(v[3] for v in STREAMS)
    tails = tuple(n - c for n, c in zip(sizes, cuts))

    def ring(rows, dtype):
        first = both((4, rows), F32, sizes) + (both((4, rows), BF, sizes) if dtype == BF else [])
        return (first + both((rows,), dtype, cuts) + both((rows,), dtype, tails)
                + both((rows,), dtype, sizes) + both((rows,), dtype, sizes)
                + both((rows,), dtype, cuts) + both((rows,), dtype, tails))

    dacts, dw = pl.pallas_call(
        lambda *refs: kernel(n_norm, *refs),
        out_shape=(jax.ShapeDtypeStruct((2, 64, 384), BF),
                   jax.ShapeDtypeStruct((2, 36, 8, 128), BF)),
        in_specs=[pl.BlockSpec(memory_space=pltpu.HBM)] * 5,
        out_specs=(vm, vm),
        scratch_shapes=[
            VMEM((2, 2, 192, 128), BF), VMEM((12, 27, 192), BF), VMEM((384,), F32),
            VMEM((384,), F32), pltpu.SemaphoreType.DMA((6,)),
            VMEM((2, 2, 64, 384), BF), VMEM((6, 6, 96, 128), BF),
            VMEM((2, 1, 128), F32), VMEM((2, 15, 1, 128), F32),
            VMEM((TAPK, 768), BF), VMEM((TAPK, 768), BF),
            VMEM((2, 192, 256), BF), VMEM((2, 192, 256), BF),
            VMEM((16, 3 * TAPK), F32),
            *both((4, 16), BF), *both((4, 48), BF), *ring(48, BF), *ring(12, F32),
            VMEM((20, 8, 128), F32), VMEM((16, 8, 128), F32),
            VMEM((3, 5, 8, 128), F32), VMEM((3, 4, 8, 128), F32),
            VMEM((3, 5, 8, 128), BF), VMEM((3, 4, 8, 128), BF),
            VMEM((3, 5, 8, 128), BF), VMEM((3, 4, 8, 128), BF),
            VMEM((5, 8, 128), BF), VMEM((4, 8, 128), BF),
            VMEM((2, 20, 8, 128), BF), VMEM((2, 16, 8, 128), BF),
            VMEM((2, 192, 256), F32), VMEM((192, 256), F32), VMEM((192, 512), F32),
            VMEM((2, 2, 64, 384), BF), VMEM((2, 64, 384), BF),
            dma, dma,
        ],
        compiler_params=pltpu.CompilerParams(
            collective_id=0, has_side_effects=True, vmem_limit_bytes=20 * 1024 * 1024),
        name="backward",
    )(*(pltpu.with_memory_space_constraint(v, pltpu.HBM) for v in (acts2, cot, weights, gamma, beta)))
    dacts, dw = pl.pallas_call(
        finish,
        out_shape=(jax.ShapeDtypeStruct((2, 64, 384), BF),
                   jax.ShapeDtypeStruct((12, 27, 192), F32)),
        in_specs=[vm] * 2,
        out_specs=(vm, vm),
        scratch_shapes=[VMEM((2, 16, 3 * TAPK), F32)],
        compiler_params=pltpu.CompilerParams(vmem_limit_bytes=8 * 1024 * 1024),
        name="finish",
    )(dacts, dw)
    return dacts.reshape(2, 1, 64, 384), dw


def solution(mesh):
    placed = (
        P("block", "tile", None, None),
        P(),
        P(),
        P("tile", None, None),
        P("block", "tile", None, None),
    )
    return jax.shard_map(
        shards,
        mesh=mesh,
        in_specs=placed,
        out_specs=(P("block", "tile", None, None), P("tile", None, None)),
        check_vma=False,
    )
```
